256 devices in a mesh: chan: 8 (over x_hi, y), tm: 32 (over x_lo, z, core).
Axes of the slice: x: 4 (x_hi: 2, x_lo: 2; x = x_hi * 2 + x_lo), y: 4, z: 8, core: 2. Of those that a mesh axis runs over, the one named last changes fastest.
Arguments:
- records: bfloat16 [1408, 1024, 1024], P('tm', 'chan'), may hold values from -2000 to 2000, as said below
Outputs:
- cross_near: float32 [32, 2, 4, 1024, 2, 128], P('tm', None, None, 'chan')
- cross_far: float32 [32, 1024, 2, 128], P('tm', 'chan')
The draws below stay inside these ranges and needn't reach their ends.
Inputs may be any that keep to these rules, and one draw needn't show every extreme that they name: Raw strain-rate records.
All inputs are finite; a program needn't handle non-finite values.
Results may differ from the reference program's by a relative error of at most 0.009.
Values may be sent and summed in bfloat16 or wider, within the bound.
A program may use at most 128 MiB of HBM per device.

```python
import math
import jax
import jax.numpy as jnp
from jax import lax

CH_DEV = 128
CHANNELS = 1024
FREQS = 64
SAMPLES = 1024
FIRST_BIN = 32
W_DEV = 44
WINDOWS = 1408
HALF = 4
N_TM = 32


def draw_records(key, part):
    noise_key = jax.random.fold_in(key, 11)
    channel_key = jax.random.fold_in(key, 12)
    window_key = jax.random.fold_in(key, 13)
    channel_scale = jnp.exp(jax.random.uniform(channel_key, (1, CHANNELS, 1), jnp.float32, 0.0, math.log(10.0)))
    window_scale = jnp.exp(jax.random.uniform(window_key, (WINDOWS, 1, 1), jnp.float32, 0.0, math.log(10.0)))
    base = jax.random.normal(noise_key, (WINDOWS, CHANNELS, SAMPLES), jnp.float32)
    base = jnp.clip(base, -6.0, 6.0)
    return (base * channel_scale * window_scale).astype(jnp.bfloat16)


def setup_inputs(seed: int = 0) -> dict:
    key_of = jax.random.split(jax.random.key(seed), 2)
    records = draw_records(jax.random.fold_in(key_of[1], 71), 0)
    return {"records": records}


EPSILON = 1e-06

def dft_table(sample_count, frequency_count, first_bin):
    positions = jnp.arange(sample_count, dtype=jnp.int32)
    bin_numbers = jnp.arange(frequency_count, dtype=jnp.int32) + first_bin
    phase_index = bin_numbers[:, None] * positions[None, :] % sample_count
    phase_angle = 2.0 * math.pi / sample_count * phase_index.astype(jnp.float32)
    hann_taper = 0.5 - 0.5 * jnp.cos(2.0 * math.pi / sample_count * positions.astype(jnp.float32))
    cosine = hann_taper[None, :] * jnp.cos(phase_angle)
    sine_part = -hann_taper[None, :] * jnp.sin(phase_angle)
    return jnp.stack([cosine, sine_part], axis=1).reshape(2 * frequency_count, sample_count).astype(jnp.bfloat16)

def whiten(records, taper_table, overall_scale):
    spectra = jnp.einsum('ks,wcs->kwc', taper_table.astype(jnp.float32), records.astype(jnp.float32))
    mean_square = lax.optimization_barrier(jnp.mean(spectra * spectra, axis=0))
    factor = overall_scale / jnp.sqrt(mean_square + EPSILON)
    return (spectra * factor[None]).astype(jnp.bfloat16)

def make_rows(blocks):
    negated = jnp.stack([blocks[:, :, 1], -blocks[:, :, 0]], axis=2)
    joined = jnp.stack([blocks, negated], axis=-1)
    return joined.reshape(blocks.shape[:-1] + (2 * blocks.shape[-1],))

def pair_product(row_side, column_side):
    product = jnp.einsum('hgpwai,hgpwaj->ghaij', row_side, column_side)
    rounded = lax.optimization_barrier(product.astype(jnp.bfloat16))
    return rounded.astype(jnp.float32)

def reference(records):
    taper_table = dft_table(SAMPLES, FREQS, FIRST_BIN)
    block_count = CHANNELS // CH_DEV
    half_freq = FREQS // 2
    overall_scale = WINDOWS ** (-0.25)
    lower_mask = (jnp.arange(block_count) < HALF)[None, :, None, None]

    def accumulate(carry, group_records):
        near_sum, far_sum = carry
        whitened = whiten(group_records, taper_table, overall_scale)
        blocks = whitened.reshape(2, half_freq, 2, W_DEV, block_count, CH_DEV).astype(jnp.float32)
        row_side = make_rows(blocks)
        rounds = []
        for offset in range(HALF):
            rounds.append(pair_product(row_side, jnp.roll(blocks, -offset, axis=4)))
        near_part = jnp.stack(rounds, axis=2)
        low_part = pair_product(row_side, jnp.roll(blocks, -HALF, axis=4))[:, 0]
        high_part = pair_product(jnp.roll(row_side, -HALF, axis=4), blocks)[:, 1]
        far_part = jnp.where(lower_mask, low_part, high_part)
        return ((near_sum + near_part, far_sum + far_part), None)
    near_zero = jnp.zeros((half_freq, 2, HALF, block_count, 2 * CH_DEV, CH_DEV), jnp.float32)
    far_zero = jnp.zeros((half_freq, block_count, 2 * CH_DEV, CH_DEV), jnp.float32)
    grouped = records.reshape(N_TM, W_DEV, CHANNELS, SAMPLES)
    (near_sum, far_sum), unused = lax.scan(accumulate, (near_zero, far_zero), grouped)
    cross_near = near_sum.reshape(half_freq, 2, HALF, CHANNELS, 2, CH_DEV)
    cross_far = far_sum.reshape(half_freq, CHANNELS, 2, CH_DEV)
    return (cross_near, cross_far)
```

```python
import functools
import math

import jax
import jax.numpy as jnp
from jax import lax
from jax.experimental import pallas as pl
from jax.experimental.pallas import tpu as pltpu
from jax.sharding import PartitionSpec as P

FREQS = 64
FIRST_BIN = 32
EPSILON = 1e-06
GROUPS_PER_STEP = 8


def shifted(value, axis, steps):
    count = lax.axis_size(axis)
    pairs = [(source, (source + steps) % count) for source in range(count)]
    return lax.ppermute(value, axis, pairs)


def dft_table(sample_count, frequency_count, first_bin):
    positions = jnp.arange(sample_count, dtype=jnp.int32)
    bin_numbers = jnp.arange(frequency_count, dtype=jnp.int32) + first_bin
    phase_index = bin_numbers[:, None] * positions[None, :] % sample_count
    phase_angle = 2.0 * math.pi / sample_count * phase_index.astype(jnp.float32)
    hann_taper = 0.5 - 0.5 * jnp.cos(2.0 * math.pi / sample_count * positions.astype(jnp.float32))
    cosine = hann_taper[None, :] * jnp.cos(phase_angle)
    sine_part = -hann_taper[None, :] * jnp.sin(phase_angle)
    return (
        jnp.stack([cosine, sine_part], axis=1)
        .reshape(2 * frequency_count, sample_count)
        .astype(jnp.bfloat16)
    )


def whiten(records, taper_table, overall_scale):
    spectra = jnp.einsum("ks,wcs->kwc", taper_table, records, preferred_element_type=jnp.float32)
    mean_square = jnp.mean(spectra * spectra, axis=0)
    factor = overall_scale / jnp.sqrt(mean_square + EPSILON)
    return (spectra * factor[None]).astype(jnp.bfloat16)


def row_side(blocks):
    real, imag = blocks[..., 0, :, :], blocks[..., 1, :, :]
    turned = jnp.stack([imag, -real], axis=-3)
    both = jnp.stack([blocks, turned], axis=-4)
    lead = blocks.shape[:-3]
    width, chans = blocks.shape[-2], blocks.shape[-1]
    order = tuple(range(len(lead))) + tuple(len(lead) + d for d in (0, 3, 1, 2))
    return both.transpose(order).reshape(lead + (2 * chans, 2 * width))


def pair_kernel(lhs_ref, rhs_ref, out_ref):
    chans = out_ref.shape[1]

    @pl.when(pl.program_id(1) == 0)
    def _():
        out_ref[...] = jnp.zeros_like(out_ref)

    acc = out_ref[0]
    for group in range(lhs_ref.shape[1]):
        part = jnp.dot(lhs_ref[0, group], rhs_ref[0, group], preferred_element_type=jnp.float32)
        part = part.astype(jnp.bfloat16).astype(jnp.float32)
        acc = acc + jnp.concatenate([part[:chans], part[chans:]], axis=1)
    out_ref[0] = acc


def pair_stack(lhs, rhs):
    halves, groups, rows, depth = lhs.shape
    chans = rhs.shape[-1]
    step = GROUPS_PER_STEP
    return pl.pallas_call(
        pair_kernel,
        out_shape=jax.ShapeDtypeStruct((halves, chans, 2 * chans), jnp.float32),
        grid=(halves, groups // step),
        in_specs=[
            pl.BlockSpec((1, step, rows, depth), lambda h, n: (h, n, 0, 0)),
            pl.BlockSpec((1, step, depth, chans), lambda h, n: (h, n, 0, 0)),
        ],
        out_specs=pl.BlockSpec((1, chans, 2 * chans), lambda h, n: (h, 0, 0)),
        cost_estimate=pl.CostEstimate(
            flops=2 * halves * groups * rows * depth * chans,
            bytes_accessed=2 * halves * groups * depth * (rows + chans) + 4 * halves * chans * 2 * chans,
            transcendentals=0,
        ),
    )(lhs, rhs)


def body(records):
    window_count = records.shape[0]
    chans = records.shape[1]
    time_count = lax.axis_size("tm")
    chan_count = lax.axis_size("chan")
    half_count = chan_count // 2
    taper_table = dft_table(records.shape[2], FREQS, FIRST_BIN)
    whitened = whiten(records, taper_table, float(window_count * time_count) ** (-0.25))
    half_freq = FREQS // 2
    blocks = whitened.reshape(2, half_freq, 2, window_count, chans)
    blocks = lax.all_to_all(blocks, "tm", split_axis=1, concat_axis=1, tiled=True)
    depth = 2 * window_count
    rhs_own = blocks.reshape(2, time_count, depth, chans)
    lhs_own = row_side(blocks)

    lower_half = lax.axis_index("chan") < half_count
    send_half = jnp.where(lower_half, 1, 0).astype(jnp.int32)
    far_send = lax.dynamic_slice_in_dim(blocks, send_half, 1, 0)
    far_recv = shifted(far_send, "chan", -half_count)
    mates = [shifted(rhs_own, "chan", -offset) for offset in range(1, half_count)]

    near = [pair_stack(lhs_own, rhs_own)]
    for mate in mates:
        near.append(pair_stack(lhs_own, mate))
    cross_near = jnp.stack(near, axis=1).reshape(1, 2, half_count, chans, 2, chans)

    far_lhs = jnp.where(lower_half, lhs_own[:1], row_side(far_recv))
    far_rhs = jnp.where(lower_half, far_recv.reshape(1, time_count, depth, chans), rhs_own[1:])
    cross_far = pair_stack(far_lhs, far_rhs).reshape(1, chans, 2, chans)
    return (cross_near, cross_far)


def solution(mesh):
    return jax.shard_map(
        body,
        mesh=mesh,
        in_specs=(P("tm", "chan", None),),
        out_specs=(P("tm", None, None, "chan", None, None), P("tm", "chan", None, None)),
        check_vma=False,
    )
```

```python
import functools
import math

import jax
import jax.numpy as jnp
from jax import lax
from jax.experimental import pallas as pl
from jax.experimental.pallas import tpu as pltpu
from jax.sharding import PartitionSpec as P

FREQS = 64
FIRST_BIN = 32
EPSILON = 1e-06
GROUPS_PER_STEP = 8


def shifted(value, axis, steps):
    count = lax.axis_size(axis)
    pairs = [(source, (source + steps) % count) for source in range(count)]
    return lax.ppermute(value, axis, pairs)


def dft_table(sample_count, frequency_count, first_bin):
    positions = jnp.arange(sample_count, dtype=jnp.int32)
    bin_numbers = jnp.arange(frequency_count, dtype=jnp.int32) + first_bin
    phase_index = bin_numbers[:, None] * positions[None, :] % sample_count
    phase_angle = 2.0 * math.pi / sample_count * phase_index.astype(jnp.float32)
    hann_taper = 0.5 - 0.5 * jnp.cos(2.0 * math.pi / sample_count * positions.astype(jnp.float32))
    cosine = hann_taper[None, :] * jnp.cos(phase_angle)
    sine_part = -hann_taper[None, :] * jnp.sin(phase_angle)
    return (
        jnp.stack([cosine, sine_part], axis=1)
        .reshape(2 * frequency_count, sample_count)
        .astype(jnp.bfloat16)
    )


def whiten(records, taper_table, overall_scale):
    spectra = jnp.einsum("ks,wcs->kwc", taper_table, records, preferred_element_type=jnp.float32)
    mean_square = jnp.mean(spectra * spectra, axis=0)
    factor = overall_scale / jnp.sqrt(mean_square + EPSILON)
    return (spectra * factor[None]).astype(jnp.bfloat16)


def row_side(blocks):
    real, imag = blocks[..., 0, :, :], blocks[..., 1, :, :]
    turned = jnp.stack([imag, -real], axis=-3)
    both = jnp.stack([blocks, turned], axis=-4)
    lead = blocks.shape[:-3]
    width, chans = blocks.shape[-2], blocks.shape[-1]
    order = tuple(range(len(lead))) + tuple(len(lead) + d for d in (0, 3, 1, 2))
    return both.transpose(order).reshape(lead + (2 * chans, 2 * width))


def pair_kernel(lhs_ref, rhs_ref, out_ref):
    chans = out_ref.shape[1]

    @pl.when(pl.program_id(1) == 0)
    def _():
        out_ref[...] = jnp.zeros_like(out_ref)

    acc = out_ref[0]
    for group in range(lhs_ref.shape[1]):
        part = jnp.dot(lhs_ref[0, group], rhs_ref[0, group], preferred_element_type=jnp.float32)
        part = part.astype(jnp.bfloat16).astype(jnp.float32)
        acc = acc + jnp.concatenate([part[:chans], part[chans:]], axis=1)
    out_ref[0] = acc


def pair_stack(lhs, rhs):
    halves, groups, rows, depth = lhs.shape
    chans = rhs.shape[-1]
    step = GROUPS_PER_STEP
    return pl.pallas_call(
        pair_kernel,
        out_shape=jax.ShapeDtypeStruct((halves, chans, 2 * chans), jnp.float32),
        grid=(halves, groups // step),
        in_specs=[
            pl.BlockSpec((1, step, rows, depth), lambda h, n: (h, n, 0, 0)),
            pl.BlockSpec((1, step, depth, chans), lambda h, n: (h, n, 0, 0)),
        ],
        out_specs=pl.BlockSpec((1, chans, 2 * chans), lambda h, n: (h, 0, 0)),
        cost_estimate=pl.CostEstimate(
            flops=2 * halves * groups * rows * depth * chans,
            bytes_accessed=2 * halves * groups * depth * (rows + chans) + 4 * halves * chans * 2 * chans,
            transcendentals=0,
        ),
    )(lhs, rhs)


def body(records):
    window_count = records.shape[0]
    chans = records.shape[1]
    time_count = lax.axis_size("tm")
    chan_count = lax.axis_size("chan")
    half_count = chan_count // 2
    taper_table = dft_table(records.shape[2], FREQS, FIRST_BIN)
    whitened = whiten(records, taper_table, float(window_count * time_count) ** (-0.25))
    half_freq = FREQS // 2
    depth = 2 * window_count
    lower_half = lax.axis_index("chan") < half_count
    spectra = whitened.reshape(2, half_freq, 2, window_count, chans)

    near = []
    own_h = []
    far_recv = []
    for half in range(2):
        blocks = lax.all_to_all(spectra[half], "tm", split_axis=0, concat_axis=0, tiled=True)
        own_h.append(blocks)
        rhs = blocks.reshape(1, time_count, depth, chans)
        lhs = row_side(blocks)[None]
        if half == 0:
            pairs = [(s, s - half_count) for s in range(half_count, chan_count)]
        else:
            pairs = [(s, s + half_count) for s in range(half_count)]
        far_recv.append(lax.ppermute(blocks, "chan", pairs))
        rounds = [pair_stack(lhs, rhs)]
        for offset in range(1, half_count):
            rounds.append(pair_stack(lhs, shifted(rhs, "chan", -offset)))
        near.append(jnp.stack(rounds, axis=1))
    cross_near = jnp.concatenate(near, axis=0).reshape(1, 2, half_count, chans, 2, chans)

    far_lhs = jnp.where(lower_half, row_side(own_h[0]), row_side(far_recv[1]))[None]
    far_rhs = jnp.where(lower_half, far_recv[0], own_h[1]).reshape(1, time_count, depth, chans)
    cross_far = pair_stack(far_lhs, far_rhs).reshape(1, chans, 2, chans)
    return (cross_near, cross_far)


def solution(mesh):
    return jax.shard_map(
        body,
        mesh=mesh,
        in_specs=(P("tm", "chan", None),),
        out_specs=(P("tm", None, None, "chan", None, None), P("tm", "chan", None, None)),
        check_vma=False,
    )
```

```python
import functools
import math

import jax
import jax.numpy as jnp
from jax import lax
from jax.experimental import pallas as pl
from jax.experimental.pallas import tpu as pltpu
from jax.sharding import PartitionSpec as P

FREQS = 64
FIRST_BIN = 32
EPSILON = 1e-06
GROUPS_PER_STEP = 16


def shifted(value, axis, steps):
    count = lax.axis_size(axis)
    pairs = [(source, (source + steps) % count) for source in range(count)]
    return lax.ppermute(value, axis, pairs)


def dft_table(sample_count, frequency_count, first_bin):
    positions = jnp.arange(sample_count, dtype=jnp.int32)
    bin_numbers = jnp.arange(frequency_count, dtype=jnp.int32) + first_bin
    phase_index = bin_numbers[:, None] * positions[None, :] % sample_count
    phase_angle = 2.0 * math.pi / sample_count * phase_index.astype(jnp.float32)
    hann_taper = 0.5 - 0.5 * jnp.cos(2.0 * math.pi / sample_count * positions.astype(jnp.float32))
    cosine = hann_taper[None, :] * jnp.cos(phase_angle)
    sine_part = -hann_taper[None, :] * jnp.sin(phase_angle)
    return (
        jnp.stack([cosine, sine_part], axis=1)
        .reshape(2 * frequency_count, sample_count)
        .astype(jnp.bfloat16)
    )


def whiten(records, taper_table, overall_scale):
    spectra = jnp.einsum("ks,wcs->kwc", taper_table, records, preferred_element_type=jnp.float32)
    mean_square = jnp.mean(spectra * spectra, axis=0)
    factor = overall_scale / jnp.sqrt(mean_square + EPSILON)
    return (spectra * factor[None]).astype(jnp.bfloat16)


def row_side(blocks):
    real, imag = blocks[..., 0, :, :], blocks[..., 1, :, :]
    turned = jnp.stack([imag, -real], axis=-3)
    both = jnp.stack([blocks, turned], axis=-4)
    lead = blocks.shape[:-3]
    width, chans = blocks.shape[-2], blocks.shape[-1]
    order = tuple(range(len(lead))) + tuple(len(lead) + d for d in (0, 3, 1, 2))
    return both.transpose(order).reshape(lead + (2 * chans, 2 * width))


def pair_kernel(lhs_ref, rhs_ref, out_ref):
    chans = out_ref.shape[1]

    @pl.when(pl.program_id(1) == 0)
    def _():
        out_ref[...] = jnp.zeros_like(out_ref)

    def one_group(group, acc):
        part = jnp.dot(lhs_ref[0, group], rhs_ref[0, group], preferred_element_type=jnp.float32)
        part = part.astype(jnp.bfloat16).astype(jnp.float32)
        return acc + jnp.concatenate([part[:chans], part[chans:]], axis=1)

    out_ref[0] = lax.fori_loop(0, lhs_ref.shape[1], one_group, out_ref[0], unroll=2)


def pair_stack(lhs, rhs):
    halves, groups, rows, depth = lhs.shape
    chans = rhs.shape[-1]
    step = GROUPS_PER_STEP
    return pl.pallas_call(
        pair_kernel,
        out_shape=jax.ShapeDtypeStruct((halves, chans, 2 * chans), jnp.float32),
        grid=(halves, groups // step),
        in_specs=[
            pl.BlockSpec((1, step, rows, depth), lambda h, n: (h, n, 0, 0)),
            pl.BlockSpec((1, step, depth, chans), lambda h, n: (h, n, 0, 0)),
        ],
        out_specs=pl.BlockSpec((1, chans, 2 * chans), lambda h, n: (h, 0, 0)),
        cost_estimate=pl.CostEstimate(
            flops=2 * halves * groups * rows * depth * chans,
            bytes_accessed=2 * halves * groups * depth * (rows + chans) + 4 * halves * chans * 2 * chans,
            transcendentals=0,
        ),
    )(lhs, rhs)


def body(records):
    window_count = records.shape[0]
    chans = records.shape[1]
    time_count = lax.axis_size("tm")
    chan_count = lax.axis_size("chan")
    half_count = chan_count // 2
    taper_table = dft_table(records.shape[2], FREQS, FIRST_BIN)
    whitened = whiten(records, taper_table, float(window_count * time_count) ** (-0.25))
    half_freq = FREQS // 2
    depth = 2 * window_count
    lower_half = lax.axis_index("chan") < half_count
    spectra = whitened.reshape(2, half_freq, 2, window_count, chans)

    near = []
    own_h = []
    far_recv = []
    lhs_halves = []
    for half in range(2):
        blocks = lax.all_to_all(spectra[half], "tm", split_axis=0, concat_axis=0, tiled=True)
        own_h.append(blocks)
        rhs = blocks.reshape(1, time_count, depth, chans)
        lhs = row_side(blocks)[None]
        lhs_halves.append(lhs)
        if half == 0:
            pairs = [(s, s - half_count) for s in range(half_count, chan_count)]
        else:
            pairs = [(s, s + half_count) for s in range(half_count)]
        far_recv.append(lax.ppermute(blocks, "chan", pairs))
        rounds = [pair_stack(lhs, rhs)]
        for offset in range(1, half_count):
            rounds.append(pair_stack(lhs, shifted(rhs, "chan", -offset)))
        near.append(jnp.stack(rounds, axis=1))
    cross_near = jnp.concatenate(near, axis=0).reshape(1, 2, half_count, chans, 2, chans)

    far_lhs = jnp.where(lower_half, lhs_halves[0], lhs_halves[1])
    far_rhs = jnp.where(lower_half, far_recv[0], far_recv[1]).reshape(1, time_count, depth, chans)
    product = pair_stack(far_lhs, far_rhs).reshape(chans, 2, chans)
    turned = product.transpose(2, 1, 0) * jnp.array([1.0, -1.0], jnp.float32)[None, :, None]
    cross_far = jnp.where(lower_half, product, turned).reshape(1, chans, 2, chans)
    return (cross_near, cross_far)


def solution(mesh):
    return jax.shard_map(
        body,
        mesh=mesh,
        in_specs=(P("tm", "chan", None),),
        out_specs=(P("tm", None, None, "chan", None, None), P("tm", "chan", None, None)),
        check_vma=False,
    )
```

```python
import functools
import math

import jax
import jax.numpy as jnp
from jax import lax
from jax.experimental import pallas as pl
from jax.experimental.pallas import tpu as pltpu
from jax.sharding import PartitionSpec as P

FREQS = 64
FIRST_BIN = 32
EPSILON = 1e-06
GROUPS_PER_STEP = 8


def shifted(value, axis, steps):
    count = lax.axis_size(axis)
    pairs = [(source, (source + steps) % count) for source in range(count)]
    return lax.ppermute(value, axis, pairs)


def dft_table(sample_count, frequency_count, first_bin):
    positions = jnp.arange(sample_count, dtype=jnp.int32)
    bin_numbers = jnp.arange(frequency_count, dtype=jnp.int32) + first_bin
    phase_index = bin_numbers[:, None] * positions[None, :] % sample_count
    phase_angle = 2.0 * math.pi / sample_count * phase_index.astype(jnp.float32)
    hann_taper = 0.5 - 0.5 * jnp.cos(2.0 * math.pi / sample_count * positions.astype(jnp.float32))
    cosine = hann_taper[None, :] * jnp.cos(phase_angle)
    sine_part = -hann_taper[None, :] * jnp.sin(phase_angle)
    return (
        jnp.stack([cosine, sine_part], axis=1)
        .reshape(2 * frequency_count, sample_count)
        .astype(jnp.bfloat16)
    )


def whiten(records, taper_table, overall_scale):
    spectra = jnp.einsum("ks,wcs->kwc", taper_table, records, preferred_element_type=jnp.float32)
    mean_square = jnp.mean(spectra * spectra, axis=0)
    factor = overall_scale / jnp.sqrt(mean_square + EPSILON)
    return (spectra * factor[None]).astype(jnp.bfloat16)


def pair_kernel(group_count, own_ref, *refs):
    mate_refs, out_ref = refs[:-1], refs[-1]
    chans = out_ref.shape[-2]
    contract = (((0,), (0,)), ((), ()))

    @pl.when(pl.program_id(0) == 0)
    def _():
        out_ref[...] = jnp.zeros_like(out_ref)

    for group in range(group_count):
        rows = jnp.concatenate([own_ref[group, 0], own_ref[group, 1]], axis=1)
        for index, mate_ref in enumerate(mate_refs):
            cols = jnp.concatenate([mate_ref[group, 0], mate_ref[group, 1]], axis=1)
            prod = lax.dot_general(rows, cols, contract, preferred_element_type=jnp.float32)
            real = prod[:chans, :chans] + prod[chans:, chans:]
            imag = prod[chans:, :chans] - prod[:chans, chans:]
            both = jnp.concatenate([real, imag], axis=1)
            out_ref[index] += both.astype(jnp.bfloat16).astype(jnp.float32)


def pair_stack(own, mates):
    groups, _, width, chans = own.shape
    step = GROUPS_PER_STEP
    spec = pl.BlockSpec((step, 2, width, chans), lambda n: (n, 0, 0, 0))
    count = len(mates)
    return pl.pallas_call(
        functools.partial(pair_kernel, step),
        out_shape=jax.ShapeDtypeStruct((count, chans, 2 * chans), jnp.float32),
        grid=(groups // step,),
        in_specs=[spec] * (count + 1),
        out_specs=pl.BlockSpec((count, chans, 2 * chans), lambda n: (0, 0, 0)),
        cost_estimate=pl.CostEstimate(
            flops=2 * count * groups * 2 * width * 4 * chans * chans,
            bytes_accessed=2 * (count + 1) * groups * 2 * width * chans + 4 * count * chans * 2 * chans,
            transcendentals=0,
        ),
    )(own, *mates)


def body(records):
    window_count = records.shape[0]
    chans = records.shape[1]
    chan_count = lax.axis_size("chan")
    half_count = chan_count // 2
    time_count = lax.axis_size("tm")
    taper_table = dft_table(records.shape[2], FREQS, FIRST_BIN)
    whitened = whiten(records, taper_table, float(window_count * time_count) ** (-0.25))
    half_freq = FREQS // 2
    lower_half = lax.axis_index("chan") < half_count
    spectra = whitened.reshape(2, half_freq, 2, window_count, chans)

    near = []
    own_h = []
    far_recv = []
    for half in range(2):
        blocks = lax.all_to_all(spectra[half], "tm", split_axis=0, concat_axis=0, tiled=True)
        own_h.append(blocks)
        if half == 0:
            pairs = [(s, s - half_count) for s in range(half_count, chan_count)]
        else:
            pairs = [(s, s + half_count) for s in range(half_count)]
        far_recv.append(lax.ppermute(blocks, "chan", pairs))
        mates = [blocks] + [shifted(blocks, "chan", -offset) for offset in range(1, half_count)]
        near.append(pair_stack(blocks, mates))
    cross_near = jnp.stack(near, axis=0).reshape(1, 2, half_count, chans, 2, chans)

    far_own = jnp.where(lower_half, own_h[0], own_h[1])
    far_mate = jnp.where(lower_half, far_recv[0], far_recv[1])
    product = pair_stack(far_own, [far_mate]).reshape(chans, 2, chans)
    turned = product.transpose(2, 1, 0) * jnp.array([1.0, -1.0], jnp.float32)[None, :, None]
    cross_far = jnp.where(lower_half, product, turned).reshape(1, chans, 2, chans)
    return (cross_near, cross_far)


def solution(mesh):
    return jax.shard_map(
        body,
        mesh=mesh,
        in_specs=(P("tm", "chan", None),),
        out_specs=(P("tm", None, None, "chan", None, None), P("tm", "chan", None, None)),
        check_vma=False,
    )
```

```python
import functools
import math

import jax
import jax.numpy as jnp
from jax import lax
from jax.experimental import pallas as pl
from jax.experimental.pallas import tpu as pltpu
from jax.sharding import PartitionSpec as P

FREQS = 64
FIRST_BIN = 32
EPSILON = 1e-06
GROUPS_PER_STEP = 8


def shifted(value, axis, steps):
    count = lax.axis_size(axis)
    pairs = [(source, (source + steps) % count) for source in range(count)]
    return lax.ppermute(value, axis, pairs)


def dft_table(sample_count, frequency_count, first_bin):
    positions = jnp.arange(sample_count, dtype=jnp.int32)
    bin_numbers = jnp.arange(frequency_count, dtype=jnp.int32) + first_bin
    phase_index = bin_numbers[:, None] * positions[None, :] % sample_count
    phase_angle = 2.0 * math.pi / sample_count * phase_index.astype(jnp.float32)
    hann_taper = 0.5 - 0.5 * jnp.cos(2.0 * math.pi / sample_count * positions.astype(jnp.float32))
    cosine = hann_taper[None, :] * jnp.cos(phase_angle)
    sine_part = -hann_taper[None, :] * jnp.sin(phase_angle)
    return (
        jnp.stack([cosine, sine_part], axis=1)
        .reshape(2 * frequency_count, sample_count)
        .astype(jnp.bfloat16)
    )


def whiten(records, taper_table, overall_scale):
    spectra = jnp.einsum("ks,wcs->kwc", taper_table, records, preferred_element_type=jnp.float32)
    mean_square = jnp.mean(spectra * spectra, axis=0)
    factor = overall_scale / jnp.sqrt(mean_square + EPSILON)
    return (spectra * factor[None]).astype(jnp.bfloat16)


def pair_kernel(group_count, own_ref, *refs):
    mate_refs, out_ref = refs[:-1], refs[-1]
    chans = out_ref.shape[-2]
    contract = (((0,), (0,)), ((), ()))

    @pl.when(pl.program_id(0) == 0)
    def _():
        out_ref[...] = jnp.zeros_like(out_ref)

    for group in range(group_count):
        rows = jnp.concatenate([own_ref[group, 0], own_ref[group, 1]], axis=1)
        for index, mate_ref in enumerate(mate_refs):
            cols = jnp.concatenate([mate_ref[group, 0], mate_ref[group, 1]], axis=1)
            prod = lax.dot_general(rows, cols, contract, preferred_element_type=jnp.float32)
            real = prod[:chans, :chans] + prod[chans:, chans:]
            imag = prod[chans:, :chans] - prod[:chans, chans:]
            both = jnp.concatenate([real, imag], axis=1)
            out_ref[index] += both.astype(jnp.bfloat16).astype(jnp.float32)


def pair_stack(own, mates):
    groups, _, width, chans = own.shape
    step = GROUPS_PER_STEP
    spec = pl.BlockSpec((step, 2, width, chans), lambda n: (n, 0, 0, 0))
    count = len(mates)
    return pl.pallas_call(
        functools.partial(pair_kernel, step),
        out_shape=jax.ShapeDtypeStruct((count, chans, 2 * chans), jnp.float32),
        grid=(groups // step,),
        in_specs=[spec] * (count + 1),
        out_specs=pl.BlockSpec((count, chans, 2 * chans), lambda n: (0, 0, 0)),
        cost_estimate=pl.CostEstimate(
            flops=2 * count * groups * 2 * width * 4 * chans * chans,
            bytes_accessed=2 * (count + 1) * groups * 2 * width * chans + 4 * count * chans * 2 * chans,
            transcendentals=0,
        ),
    )(own, *mates)


def body(records):
    window_count = records.shape[0]
    chans = records.shape[1]
    chan_count = lax.axis_size("chan")
    half_count = chan_count // 2
    time_count = lax.axis_size("tm")
    taper_table = dft_table(records.shape[2], FREQS, FIRST_BIN)
    whitened = whiten(records, taper_table, float(window_count * time_count) ** (-0.25))
    half_freq = FREQS // 2
    lower_half = lax.axis_index("chan") < half_count
    spectra = whitened.reshape(2, half_freq, 2, window_count, chans)

    near = []
    own_h = []
    far_recv = []
    for half in range(2):
        blocks = lax.all_to_all(spectra[half], "tm", split_axis=0, concat_axis=0, tiled=True)
        own_h.append(blocks)
        if half == 0:
            pairs = [(s, s - half_count) for s in range(half_count, chan_count)]
        else:
            pairs = [(s, s + half_count) for s in range(half_count)]
        far_recv.append(lax.ppermute(blocks, "chan", pairs))
        mates = [blocks] + [shifted(blocks, "chan", -offset) for offset in range(1, half_count)]
        near.append(jnp.concatenate([pair_stack(blocks, [mate]) for mate in mates], axis=0))
    cross_near = jnp.stack(near, axis=0).reshape(1, 2, half_count, chans, 2, chans)

    far_own = jnp.where(lower_half, own_h[0], own_h[1])
    far_mate = jnp.where(lower_half, far_recv[0], far_recv[1])
    product = pair_stack(far_own, [far_mate]).reshape(chans, 2, chans)
    turned = product.transpose(2, 1, 0) * jnp.array([1.0, -1.0], jnp.float32)[None, :, None]
    cross_far = jnp.where(lower_half, product, turned).reshape(1, chans, 2, chans)
    return (cross_near, cross_far)


def solution(mesh):
    return jax.shard_map(
        body,
        mesh=mesh,
        in_specs=(P("tm", "chan", None),),
        out_specs=(P("tm", None, None, "chan", None, None), P("tm", "chan", None, None)),
        check_vma=False,
    )
```

```python
import functools
import math

import jax
import jax.numpy as jnp
from jax import lax
from jax.experimental import pallas as pl
from jax.experimental.pallas import tpu as pltpu
from jax.sharding import PartitionSpec as P

FREQS = 64
FIRST_BIN = 32
EPSILON = 1e-06
GROUPS_PER_STEP = 16


def shifted(value, axis, steps):
    count = lax.axis_size(axis)
    pairs = [(source, (source + steps) % count) for source in range(count)]
    return lax.ppermute(value, axis, pairs)


def dft_table(sample_count, frequency_count, first_bin):
    positions = jnp.arange(sample_count, dtype=jnp.int32)
    bin_numbers = jnp.arange(frequency_count, dtype=jnp.int32) + first_bin
    phase_index = bin_numbers[:, None] * positions[None, :] % sample_count
    phase_angle = 2.0 * math.pi / sample_count * phase_index.astype(jnp.float32)
    hann_taper = 0.5 - 0.5 * jnp.cos(2.0 * math.pi / sample_count * positions.astype(jnp.float32))
    cosine = hann_taper[None, :] * jnp.cos(phase_angle)
    sine_part = -hann_taper[None, :] * jnp.sin(phase_angle)
    return (
        jnp.stack([cosine, sine_part], axis=1)
        .reshape(2 * frequency_count, sample_count)
        .astype(jnp.bfloat16)
    )


def whiten(records, taper_table, overall_scale):
    spectra = jnp.einsum("ks,wcs->kwc", taper_table, records, preferred_element_type=jnp.float32)
    mean_square = jnp.mean(spectra * spectra, axis=0)
    factor = overall_scale / jnp.sqrt(mean_square + EPSILON)
    return (spectra * factor[None]).astype(jnp.bfloat16)


def pair_kernel(group_count, own_ref, *refs):
    mate_refs, out_ref = refs[:-1], refs[-1]
    chans = out_ref.shape[-2]
    contract = (((0,), (0,)), ((), ()))

    @pl.when(pl.program_id(0) == 0)
    def _():
        out_ref[...] = jnp.zeros_like(out_ref)

    for group in range(group_count):
        rows = jnp.concatenate([own_ref[group, 0], own_ref[group, 1]], axis=1)
        for index, mate_ref in enumerate(mate_refs):
            cols = jnp.concatenate([mate_ref[group, 0], mate_ref[group, 1]], axis=1)
            prod = lax.dot_general(rows, cols, contract, preferred_element_type=jnp.float32)
            real = prod[:chans, :chans] + prod[chans:, chans:]
            imag = prod[chans:, :chans] - prod[:chans, chans:]
            both = jnp.concatenate([real, imag], axis=1)
            out_ref[index] += both.astype(jnp.bfloat16).astype(jnp.float32)


def pair_stack(own, mates):
    groups, _, width, chans = own.shape
    step = GROUPS_PER_STEP
    spec = pl.BlockSpec((step, 2, width, chans), lambda n: (n, 0, 0, 0))
    count = len(mates)
    return pl.pallas_call(
        functools.partial(pair_kernel, step),
        out_shape=jax.ShapeDtypeStruct((count, chans, 2 * chans), jnp.float32),
        grid=(groups // step,),
        in_specs=[spec] * (count + 1),
        out_specs=pl.BlockSpec((count, chans, 2 * chans), lambda n: (0, 0, 0)),
        cost_estimate=pl.CostEstimate(
            flops=2 * count * groups * 2 * width * 4 * chans * chans,
            bytes_accessed=2 * (count + 1) * groups * 2 * width * chans + 4 * count * chans * 2 * chans,
            transcendentals=0,
        ),
    )(own, *mates)


def body(records):
    window_count = records.shape[0]
    chans = records.shape[1]
    chan_count = lax.axis_size("chan")
    half_count = chan_count // 2
    time_count = lax.axis_size("tm")
    taper_table = dft_table(records.shape[2], FREQS, FIRST_BIN)
    whitened = whiten(records, taper_table, float(window_count * time_count) ** (-0.25))
    half_freq = FREQS // 2
    lower_half = lax.axis_index("chan") < half_count
    spectra = whitened.reshape(2, half_freq, 2, window_count, chans)

    near = []
    own_h = []
    far_recv = []
    for half in range(2):
        blocks = lax.all_to_all(spectra[half], "tm", split_axis=0, concat_axis=0, tiled=True)
        own_h.append(blocks)
        if half == 0:
            pairs = [(s, s - half_count) for s in range(half_count, chan_count)]
        else:
            pairs = [(s, s + half_count) for s in range(half_count)]
        far_recv.append(lax.ppermute(blocks, "chan", pairs))
        mates = [blocks] + [shifted(blocks, "chan", -offset) for offset in range(1, half_count)]
        first = pair_stack(blocks, mates[:2])
        near.append(jnp.concatenate([first] + [pair_stack(blocks, [mate]) for mate in mates[2:]], axis=0))
    cross_near = jnp.stack(near, axis=0).reshape(1, 2, half_count, chans, 2, chans)

    far_own = jnp.where(lower_half, own_h[0], own_h[1])
    far_mate = jnp.where(lower_half, far_recv[0], far_recv[1])
    product = pair_stack(far_own, [far_mate]).reshape(chans, 2, chans)
    turned = product.transpose(2, 1, 0) * jnp.array([1.0, -1.0], jnp.float32)[None, :, None]
    cross_far = jnp.where(lower_half, product, turned).reshape(1, chans, 2, chans)
    return (cross_near, cross_far)


def solution(mesh):
    return jax.shard_map(
        body,
        mesh=mesh,
        in_specs=(P("tm", "chan", None),),
        out_specs=(P("tm", None, None, "chan", None, None), P("tm", "chan", None, None)),
        check_vma=False,
    )
```

```python
import functools
import math

import jax
import jax.numpy as jnp
from jax import lax
from jax.experimental import pallas as pl
from jax.experimental.pallas import tpu as pltpu
from jax.sharding import PartitionSpec as P

FREQS = 64
FIRST_BIN = 32
EPSILON = 1e-06
GROUPS_PER_STEP = 16


def shifted(value, axis, steps):
    count = lax.axis_size(axis)
    pairs = [(source, (source + steps) % count) for source in range(count)]
    return lax.ppermute(value, axis, pairs)


def dft_table(sample_count, frequency_count, first_bin):
    positions = jnp.arange(sample_count, dtype=jnp.int32)
    bin_numbers = jnp.arange(frequency_count, dtype=jnp.int32) + first_bin
    phase_index = bin_numbers[:, None] * positions[None, :] % sample_count
    phase_angle = 2.0 * math.pi / sample_count * phase_index.astype(jnp.float32)
    hann_taper = 0.5 - 0.5 * jnp.cos(2.0 * math.pi / sample_count * positions.astype(jnp.float32))
    cosine = hann_taper[None, :] * jnp.cos(phase_angle)
    sine_part = -hann_taper[None, :] * jnp.sin(phase_angle)
    return (
        jnp.stack([cosine, sine_part], axis=1)
        .reshape(2 * frequency_count, sample_count)
        .astype(jnp.bfloat16)
    )


def whiten(records, taper_table, overall_scale):
    spectra = jnp.einsum("ks,wcs->kwc", taper_table, records, preferred_element_type=jnp.float32)
    mean_square = jnp.mean(spectra * spectra, axis=0)
    factor = overall_scale / jnp.sqrt(mean_square + EPSILON)
    return (spectra * factor[None]).astype(jnp.bfloat16)


def pair_kernel(group_count, own_ref, *refs):
    mate_refs, out_ref = refs[:-1], refs[-1]
    chans = out_ref.shape[-2]
    contract = (((0,), (0,)), ((), ()))

    @pl.when(pl.program_id(0) == 0)
    def _():
        out_ref[...] = jnp.zeros_like(out_ref)

    for group in range(group_count):
        rows = jnp.concatenate([own_ref[group, 0], own_ref[group, 1]], axis=1)
        for index, mate_ref in enumerate(mate_refs):
            cols = jnp.concatenate([mate_ref[group, 0], mate_ref[group, 1]], axis=1)
            prod = lax.dot_general(rows, cols, contract, preferred_element_type=jnp.float32)
            real = prod[:chans, :chans] + prod[chans:, chans:]
            imag = prod[chans:, :chans] - prod[:chans, chans:]
            both = jnp.concatenate([real, imag], axis=1)
            out_ref[index] += both.astype(jnp.bfloat16).astype(jnp.float32)


def pair_stack(own, mates):
    groups, _, width, chans = own.shape
    step = GROUPS_PER_STEP
    spec = pl.BlockSpec((step, 2, width, chans), lambda n: (n, 0, 0, 0))
    count = len(mates)
    return pl.pallas_call(
        functools.partial(pair_kernel, step),
        out_shape=jax.ShapeDtypeStruct((count, chans, 2 * chans), jnp.float32),
        grid=(groups // step,),
        in_specs=[spec] * (count + 1),
        out_specs=pl.BlockSpec((count, chans, 2 * chans), lambda n: (0, 0, 0)),
        cost_estimate=pl.CostEstimate(
            flops=2 * count * groups * 2 * width * 4 * chans * chans,
            bytes_accessed=2 * (count + 1) * groups * 2 * width * chans + 4 * count * chans * 2 * chans,
            transcendentals=0,
        ),
    )(own, *mates)


def joint_permute(value, route):
    chan_count, time_count = lax.axis_size("chan"), lax.axis_size("tm")
    pairs = []
    for chan in range(chan_count):
        for time in range(time_count):
            target = route(chan, time)
            if target is not None:
                pairs.append((chan * time_count + time, target[0] * time_count + target[1]))
    return lax.ppermute(value, ("chan", "tm"), pairs)


def body(records):
    window_count = records.shape[0]
    chans = records.shape[1]
    chan_count = lax.axis_size("chan")
    half_count = chan_count // 2
    time_count = lax.axis_size("tm")
    half_time = time_count // 2
    taper_table = dft_table(records.shape[2], FREQS, FIRST_BIN)
    whitened = whiten(records, taper_table, float(window_count * time_count) ** (-0.25))
    half_freq = FREQS // 2
    lower_half = lax.axis_index("chan") < half_count
    spectra = whitened.reshape(2, half_freq, 2, window_count, chans)

    def upper(chan):
        return chan // half_count == 1

    def flip(time):
        return (time + half_time) % time_count

    def mate_route(offset):
        def route(chan, time):
            target = (chan - offset) % chan_count
            return (target, time if upper(target) == upper(chan) else flip(time))
        return route

    near = []
    own_h = []
    far_recv = []
    for half in range(2):
        sent = jnp.where(lower_half, spectra[half], jnp.roll(spectra[half], half_time, axis=0))
        blocks = lax.all_to_all(sent, "tm", split_axis=0, concat_axis=0, tiled=True)
        own_h.append(blocks)

        def far_route(chan, time, half=half):
            if upper(chan) == (half == 0):
                return ((chan + half_count) % chan_count, flip(time))
            return None

        far_recv.append(joint_permute(blocks, far_route))
        mates = [blocks] + [joint_permute(blocks, mate_route(offset)) for offset in range(1, half_count)]
        first = pair_stack(blocks, mates[:2])
        near.append(jnp.concatenate([first] + [pair_stack(blocks, [mate]) for mate in mates[2:]], axis=0))

    far_own = jnp.where(lower_half, own_h[0], own_h[1])
    far_mate = jnp.where(lower_half, far_recv[0], far_recv[1])
    product = pair_stack(far_own, [far_mate]).reshape(chans, 2, chans)
    turned = product.transpose(2, 1, 0) * jnp.array([1.0, -1.0], jnp.float32)[None, :, None]
    far_part = jnp.where(lower_half, product, turned)

    def home(chan, time):
        return (chan, flip(time)) if upper(chan) else None

    near = [jnp.where(lower_half, part, joint_permute(part, home)) for part in near]
    far_part = jnp.where(lower_half, far_part, joint_permute(far_part, home))
    cross_near = jnp.stack(near, axis=0).reshape(1, 2, half_count, chans, 2, chans)
    cross_far = far_part.reshape(1, chans, 2, chans)
    return (cross_near, cross_far)


def solution(mesh):
    return jax.shard_map(
        body,
        mesh=mesh,
        in_specs=(P("tm", "chan", None),),
        out_specs=(P("tm", None, None, "chan", None, None), P("tm", "chan", None, None)),
        check_vma=False,
    )
```

```python
import functools
import math

import jax
import jax.numpy as jnp
from jax import lax
from jax.experimental import pallas as pl
from jax.experimental.pallas import tpu as pltpu
from jax.sharding import PartitionSpec as P

FREQS = 64
FIRST_BIN = 32
EPSILON = 1e-06
GROUPS_PER_STEP = 32
UNROLL = 8


def shifted(value, axis, steps):
    count = lax.axis_size(axis)
    pairs = [(source, (source + steps) % count) for source in range(count)]
    return lax.ppermute(value, axis, pairs)


def dft_table(sample_count, frequency_count, first_bin):
    positions = jnp.arange(sample_count, dtype=jnp.int32)
    bin_numbers = jnp.arange(frequency_count, dtype=jnp.int32) + first_bin
    phase_index = bin_numbers[:, None] * positions[None, :] % sample_count
    phase_angle = 2.0 * math.pi / sample_count * phase_index.astype(jnp.float32)
    hann_taper = 0.5 - 0.5 * jnp.cos(2.0 * math.pi / sample_count * positions.astype(jnp.float32))
    cosine = hann_taper[None, :] * jnp.cos(phase_angle)
    sine_part = -hann_taper[None, :] * jnp.sin(phase_angle)
    return (
        jnp.stack([cosine, sine_part], axis=1)
        .reshape(2 * frequency_count, sample_count)
        .astype(jnp.bfloat16)
    )


def whiten(records, taper_table, overall_scale):
    spectra = jnp.einsum("ks,wcs->kwc", taper_table, records, preferred_element_type=jnp.float32)
    mean_square = jnp.mean(spectra * spectra, axis=0)
    factor = overall_scale / jnp.sqrt(mean_square + EPSILON)
    return (spectra * factor[None]).astype(jnp.bfloat16)


def pair_kernel(group_count, own_ref, *refs):
    mate_refs, out_ref = refs[:-1], refs[-1]
    chans = out_ref.shape[-2]
    contract = (((0,), (0,)), ((), ()))

    @pl.when(pl.program_id(0) == 0)
    def _():
        out_ref[...] = jnp.zeros_like(out_ref)

    def chunk(index, carry):
        for offset in range(UNROLL):
            group = index * UNROLL + offset
            rows = jnp.concatenate([own_ref[group, 0], own_ref[group, 1]], axis=1)
            for slot, mate_ref in enumerate(mate_refs):
                cols = jnp.concatenate([mate_ref[group, 0], mate_ref[group, 1]], axis=1)
                prod = lax.dot_general(rows, cols, contract, preferred_element_type=jnp.float32)
                real = prod[:chans, :chans] + prod[chans:, chans:]
                imag = prod[chans:, :chans] - prod[:chans, chans:]
                both = jnp.concatenate([real, imag], axis=1)
                out_ref[slot] += both.astype(jnp.bfloat16).astype(jnp.float32)
        return carry

    lax.fori_loop(0, group_count // UNROLL, chunk, 0)


def pair_stack(own, mates):
    groups, _, width, chans = own.shape
    step = GROUPS_PER_STEP
    spec = pl.BlockSpec((step, 2, width, chans), lambda n: (n, 0, 0, 0))
    count = len(mates)
    return pl.pallas_call(
        functools.partial(pair_kernel, step),
        out_shape=jax.ShapeDtypeStruct((count, chans, 2 * chans), jnp.float32),
        grid=(groups // step,),
        in_specs=[spec] * (count + 1),
        out_specs=pl.BlockSpec((count, chans, 2 * chans), lambda n: (0, 0, 0)),
        cost_estimate=pl.CostEstimate(
            flops=2 * count * groups * 2 * width * 4 * chans * chans,
            bytes_accessed=2 * (count + 1) * groups * 2 * width * chans + 4 * count * chans * 2 * chans,
            transcendentals=0,
        ),
    )(own, *mates)


def body(records):
    window_count = records.shape[0]
    chans = records.shape[1]
    chan_count = lax.axis_size("chan")
    half_count = chan_count // 2
    time_count = lax.axis_size("tm")
    taper_table = dft_table(records.shape[2], FREQS, FIRST_BIN)
    whitened = whiten(records, taper_table, float(window_count * time_count) ** (-0.25))
    half_freq = FREQS // 2
    lower_half = lax.axis_index("chan") < half_count
    spectra = whitened.reshape(2, half_freq, 2, window_count, chans)

    near = []
    own_h = []
    far_recv = []
    for half in range(2):
        blocks = lax.all_to_all(spectra[half], "tm", split_axis=0, concat_axis=0, tiled=True)
        own_h.append(blocks)
        if half == 0:
            pairs = [(s, s - half_count) for s in range(half_count, chan_count)]
        else:
            pairs = [(s, s + half_count) for s in range(half_count)]
        far_recv.append(lax.ppermute(blocks, "chan", pairs))
        mates = [blocks] + [shifted(blocks, "chan", -offset) for offset in range(1, half_count)]
        first = pair_stack(blocks, mates[:2])
        near.append(jnp.concatenate([first] + [pair_stack(blocks, [mate]) for mate in mates[2:]], axis=0))
    cross_near = jnp.stack(near, axis=0).reshape(1, 2, half_count, chans, 2, chans)

    far_own = jnp.where(lower_half, own_h[0], own_h[1])
    far_mate = jnp.where(lower_half, far_recv[0], far_recv[1])
    product = pair_stack(far_own, [far_mate]).reshape(chans, 2, chans)
    turned = product.transpose(2, 1, 0) * jnp.array([1.0, -1.0], jnp.float32)[None, :, None]
    cross_far = jnp.where(lower_half, product, turned).reshape(1, chans, 2, chans)
    return (cross_near, cross_far)


def solution(mesh):
    return jax.shard_map(
        body,
        mesh=mesh,
        in_specs=(P("tm", "chan", None),),
        out_specs=(P("tm", None, None, "chan", None, None), P("tm", "chan", None, None)),
        check_vma=False,
    )
```

```python
import functools
import math

import jax
import ml_dtypes
import numpy as np
import jax.numpy as jnp
from jax import lax
from jax.experimental import pallas as pl
from jax.experimental.pallas import tpu as pltpu
from jax.sharding import PartitionSpec as P

FREQS = 64
FIRST_BIN = 32
EPSILON = 1e-06
GROUPS_PER_STEP = 16


def shifted(value, axis, steps):
    count = lax.axis_size(axis)
    pairs = [(source, (source + steps) % count) for source in range(count)]
    return lax.ppermute(value, axis, pairs)


def dft_table(sample_count, frequency_count, first_bin):
    positions = np.arange(sample_count, dtype=np.int64)
    bin_numbers = np.arange(frequency_count, dtype=np.int64) + first_bin
    phase_index = bin_numbers[:, None] * positions[None, :] % sample_count
    phase_angle = 2.0 * math.pi / sample_count * phase_index
    hann_taper = 0.5 - 0.5 * np.cos(2.0 * math.pi / sample_count * positions)
    cosine = hann_taper[None, :] * np.cos(phase_angle)
    sine_part = -hann_taper[None, :] * np.sin(phase_angle)
    table = np.stack([cosine, sine_part], axis=1).reshape(2 * frequency_count, sample_count)
    return jnp.asarray(table.astype(np.float32).astype(ml_dtypes.bfloat16))


def whiten(records, taper_table, overall_scale):
    spectra = jnp.einsum("ks,wcs->kwc", taper_table, records, preferred_element_type=jnp.float32)
    mean_square = jnp.mean(spectra * spectra, axis=0)
    factor = overall_scale / jnp.sqrt(mean_square + EPSILON)
    return (spectra * factor[None]).astype(jnp.bfloat16)


def pair_kernel(group_count, own_ref, *refs):
    mate_refs, out_ref = refs[:-1], refs[-1]
    chans = out_ref.shape[-2]
    contract = (((0,), (0,)), ((), ()))

    @pl.when(pl.program_id(0) == 0)
    def _():
        out_ref[...] = jnp.zeros_like(out_ref)

    for group in range(group_count):
        rows = jnp.concatenate([own_ref[group, 0], own_ref[group, 1]], axis=1)
        for index, mate_ref in enumerate(mate_refs):
            cols = jnp.concatenate([mate_ref[group, 0], mate_ref[group, 1]], axis=1)
            prod = lax.dot_general(rows, cols, contract, preferred_element_type=jnp.float32)
            real = prod[:chans, :chans] + prod[chans:, chans:]
            imag = prod[chans:, :chans] - prod[:chans, chans:]
            both = jnp.concatenate([real, imag], axis=1)
            out_ref[index] += both.astype(jnp.bfloat16).astype(jnp.float32)


def pair_stack(own, mates):
    groups, _, width, chans = own.shape
    step = GROUPS_PER_STEP
    spec = pl.BlockSpec((step, 2, width, chans), lambda n: (n, 0, 0, 0))
    count = len(mates)
    return pl.pallas_call(
        functools.partial(pair_kernel, step),
        out_shape=jax.ShapeDtypeStruct((count, chans, 2 * chans), jnp.float32),
        grid=(groups // step,),
        in_specs=[spec] * (count + 1),
        out_specs=pl.BlockSpec((count, chans, 2 * chans), lambda n: (0, 0, 0)),
        cost_estimate=pl.CostEstimate(
            flops=2 * count * groups * 2 * width * 4 * chans * chans,
            bytes_accessed=2 * (count + 1) * groups * 2 * width * chans + 4 * count * chans * 2 * chans,
            transcendentals=0,
        ),
    )(own, *mates)


def body(records):
    window_count = records.shape[0]
    chans = records.shape[1]
    chan_count = lax.axis_size("chan")
    half_count = chan_count // 2
    time_count = lax.axis_size("tm")
    taper_table = dft_table(records.shape[2], FREQS, FIRST_BIN)
    whitened = whiten(records, taper_table, float(window_count * time_count) ** (-0.25))
    half_freq = FREQS // 2
    lower_half = lax.axis_index("chan") < half_count
    spectra = whitened.reshape(2, half_freq, 2, window_count, chans)

    near = []
    own_h = []
    far_recv = []
    for half in range(2):
        blocks = lax.all_to_all(spectra[half], "tm", split_axis=0, concat_axis=0, tiled=True)
        own_h.append(blocks)
        if half == 0:
            pairs = [(s, s - half_count) for s in range(half_count, chan_count)]
        else:
            pairs = [(s, s + half_count) for s in range(half_count)]
        far_recv.append(lax.ppermute(blocks, "chan", pairs))
        mates = [blocks] + [shifted(blocks, "chan", -offset) for offset in range(1, half_count)]
        first = pair_stack(blocks, mates[:2])
        near.append(jnp.concatenate([first] + [pair_stack(blocks, [mate]) for mate in mates[2:]], axis=0))
    cross_near = jnp.stack(near, axis=0).reshape(1, 2, half_count, chans, 2, chans)

    far_own = jnp.where(lower_half, own_h[0], own_h[1])
    far_mate = jnp.where(lower_half, far_recv[0], far_recv[1])
    product = pair_stack(far_own, [far_mate]).reshape(chans, 2, chans)
    turned = product.transpose(2, 1, 0) * jnp.array([1.0, -1.0], jnp.float32)[None, :, None]
    cross_far = jnp.where(lower_half, product, turned).reshape(1, chans, 2, chans)
    return (cross_near, cross_far)


def solution(mesh):
    return jax.shard_map(
        body,
        mesh=mesh,
        in_specs=(P("tm", "chan", None),),
        out_specs=(P("tm", None, None, "chan", None, None), P("tm", "chan", None, None)),
        check_vma=False,
    )
```

```python
import functools
import math

import jax
import ml_dtypes
import numpy as np
import jax.numpy as jnp
from jax import lax
from jax.experimental import pallas as pl
from jax.experimental.pallas import tpu as pltpu
from jax.sharding import PartitionSpec as P

FREQS = 64
FIRST_BIN = 32
EPSILON = 1e-06
GROUPS_PER_STEP = 16


def shifted(value, axis, steps):
    count = lax.axis_size(axis)
    pairs = [(source, (source + steps) % count) for source in range(count)]
    return lax.ppermute(value, axis, pairs)


def dft_table(sample_count, frequency_count, first_bin):
    positions = np.arange(sample_count, dtype=np.int64)
    bin_numbers = np.arange(frequency_count, dtype=np.int64) + first_bin
    phase_index = bin_numbers[:, None] * positions[None, :] % sample_count
    phase_angle = 2.0 * math.pi / sample_count * phase_index
    hann_taper = 0.5 - 0.5 * np.cos(2.0 * math.pi / sample_count * positions)
    cosine = hann_taper[None, :] * np.cos(phase_angle)
    sine_part = -hann_taper[None, :] * np.sin(phase_angle)
    table = np.stack([cosine, sine_part], axis=1).reshape(2 * frequency_count, sample_count)
    return jnp.asarray(table.astype(np.float32).astype(ml_dtypes.bfloat16))


def whiten(records, taper_table, overall_scale):
    spectra = jnp.einsum("ks,wcs->kwc", taper_table, records, preferred_element_type=jnp.float32)
    mean_square = jnp.mean(spectra * spectra, axis=0)
    factor = overall_scale / jnp.sqrt(mean_square + EPSILON)
    return (spectra * factor[None]).astype(jnp.bfloat16)


def pair_kernel(group_count, turn, own_ref, *refs):
    mate_refs, out_ref = refs[:-1], refs[-1]
    chans = out_ref.shape[-2]
    contract = (((0,), (0,)), ((), ()))

    @pl.when(pl.program_id(0) == 0)
    def _():
        out_ref[...] = jnp.zeros_like(out_ref)

    for group in range(group_count):
        rows = jnp.concatenate([own_ref[group, 0], own_ref[group, 1]], axis=1)
        for index, mate_ref in enumerate(mate_refs):
            cols = jnp.concatenate([mate_ref[group, 0], mate_ref[group, 1]], axis=1)
            prod = lax.dot_general(rows, cols, contract, preferred_element_type=jnp.float32)
            real = prod[:chans, :chans] + prod[chans:, chans:]
            imag = prod[chans:, :chans] - prod[:chans, chans:]
            both = jnp.concatenate([real, imag], axis=1)
            out_ref[index] += both.astype(jnp.bfloat16).astype(jnp.float32)

    if turn:
        upper = lax.axis_index("chan") >= lax.axis_size("chan") // 2

        @pl.when(jnp.logical_and(upper, pl.program_id(0) == pl.num_programs(0) - 1))
        def _():
            real = out_ref[0, :, :chans]
            imag = out_ref[0, :, chans:]
            out_ref[0] = jnp.concatenate([real.T, -imag.T], axis=1)


def pair_stack(own, mates, turn=False):
    groups, _, width, chans = own.shape
    step = GROUPS_PER_STEP
    spec = pl.BlockSpec((step, 2, width, chans), lambda n: (n, 0, 0, 0))
    count = len(mates)
    return pl.pallas_call(
        functools.partial(pair_kernel, step, turn),
        out_shape=jax.ShapeDtypeStruct((count, chans, 2 * chans), jnp.float32),
        grid=(groups // step,),
        in_specs=[spec] * (count + 1),
        out_specs=pl.BlockSpec((count, chans, 2 * chans), lambda n: (0, 0, 0)),
        cost_estimate=pl.CostEstimate(
            flops=2 * count * groups * 2 * width * 4 * chans * chans,
            bytes_accessed=2 * (count + 1) * groups * 2 * width * chans + 4 * count * chans * 2 * chans,
            transcendentals=0,
        ),
    )(own, *mates)


def body(records):
    window_count = records.shape[0]
    chans = records.shape[1]
    chan_count = lax.axis_size("chan")
    half_count = chan_count // 2
    time_count = lax.axis_size("tm")
    taper_table = dft_table(records.shape[2], FREQS, FIRST_BIN)
    whitened = whiten(records, taper_table, float(window_count * time_count) ** (-0.25))
    half_freq = FREQS // 2
    lower_half = lax.axis_index("chan") < half_count
    spectra = whitened.reshape(2, half_freq, 2, window_count, chans)

    near = []
    own_h = []
    far_recv = []
    for half in range(2):
        blocks = lax.all_to_all(spectra[half], "tm", split_axis=0, concat_axis=0, tiled=True)
        own_h.append(blocks)
        if half == 0:
            pairs = [(s, s - half_count) for s in range(half_count, chan_count)]
        else:
            pairs = [(s, s + half_count) for s in range(half_count)]
        far_recv.append(lax.ppermute(blocks, "chan", pairs))
        mates = [blocks] + [shifted(blocks, "chan", -offset) for offset in range(1, half_count)]
        first = pair_stack(blocks, mates[:2])
        near.append(jnp.concatenate([first] + [pair_stack(blocks, [mate]) for mate in mates[2:]], axis=0))
    cross_near = jnp.stack(near, axis=0).reshape(1, 2, half_count, chans, 2, chans)

    far_own = jnp.where(lower_half, own_h[0], own_h[1])
    far_mate = jnp.where(lower_half, far_recv[0], far_recv[1])
    cross_far = pair_stack(far_own, [far_mate], turn=True).reshape(1, chans, 2, chans)
    return (cross_near, cross_far)


def solution(mesh):
    return jax.shard_map(
        body,
        mesh=mesh,
        in_specs=(P("tm", "chan", None),),
        out_specs=(P("tm", None, None, "chan", None, None), P("tm", "chan", None, None)),
        check_vma=False,
    )
```

```python
import functools
import math

import jax
import ml_dtypes
import numpy as np
import jax.numpy as jnp
from jax import lax
from jax.experimental import pallas as pl
from jax.experimental.pallas import tpu as pltpu
from jax.sharding import PartitionSpec as P

FREQS = 64
FIRST_BIN = 32
EPSILON = 1e-06
GROUPS_PER_STEP = 16


def shifted(value, axis, steps):
    count = lax.axis_size(axis)
    pairs = [(source, (source + steps) % count) for source in range(count)]
    return lax.ppermute(value, axis, pairs)


def dft_table(sample_count, frequency_count, first_bin):
    positions = np.arange(sample_count, dtype=np.int64)
    bin_numbers = np.arange(frequency_count, dtype=np.int64) + first_bin
    phase_index = bin_numbers[:, None] * positions[None, :] % sample_count
    phase_angle = 2.0 * math.pi / sample_count * phase_index
    hann_taper = 0.5 - 0.5 * np.cos(2.0 * math.pi / sample_count * positions)
    cosine = hann_taper[None, :] * np.cos(phase_angle)
    sine_part = -hann_taper[None, :] * np.sin(phase_angle)
    table = np.stack([cosine, sine_part], axis=1).reshape(2 * frequency_count, sample_count)
    return jnp.asarray(table.astype(np.float32).astype(ml_dtypes.bfloat16))


def whiten(records, taper_table, overall_scale):
    spectra = jnp.einsum("ks,wcs->kwc", taper_table, records, preferred_element_type=jnp.float32)
    mean_square = jnp.mean(spectra * spectra, axis=0)
    factor = overall_scale / jnp.sqrt(mean_square + EPSILON)
    return (spectra * factor[None]).astype(jnp.bfloat16)


def pair_kernel(group_count, turn, own_ref, *refs):
    mate_refs, out_ref = refs[:-1], refs[-1]
    chans = out_ref.shape[-2]
    contract = (((0,), (0,)), ((), ()))

    @pl.when(pl.program_id(0) == 0)
    def _():
        out_ref[...] = jnp.zeros_like(out_ref)

    for group in range(group_count):
        rows = jnp.concatenate([own_ref[group, 0], own_ref[group, 1]], axis=1)
        for index, mate_ref in enumerate(mate_refs):
            cols = jnp.concatenate([mate_ref[group, 0], mate_ref[group, 1]], axis=1)
            prod = lax.dot_general(rows, cols, contract, preferred_element_type=jnp.float32)
            real = prod[:chans, :chans] + prod[chans:, chans:]
            imag = prod[chans:, :chans] - prod[:chans, chans:]
            both = jnp.concatenate([real, imag], axis=1)
            out_ref[index] += both.astype(jnp.bfloat16).astype(jnp.float32)

    if turn:
        upper = lax.axis_index("chan") >= lax.axis_size("chan") // 2

        @pl.when(jnp.logical_and(upper, pl.program_id(0) == pl.num_programs(0) - 1))
        def _():
            last = len(mate_refs) - 1
            real = out_ref[last, :, :chans]
            imag = out_ref[last, :, chans:]
            out_ref[last] = jnp.concatenate([real.T, -imag.T], axis=1)


def pair_stack(own, mates, turn=False):
    groups, _, width, chans = own.shape
    step = GROUPS_PER_STEP
    spec = pl.BlockSpec((step, 2, width, chans), lambda n: (n, 0, 0, 0))
    count = len(mates)
    return pl.pallas_call(
        functools.partial(pair_kernel, step, turn),
        out_shape=jax.ShapeDtypeStruct((count, chans, 2 * chans), jnp.float32),
        grid=(groups // step,),
        in_specs=[spec] * (count + 1),
        out_specs=pl.BlockSpec((count, chans, 2 * chans), lambda n: (0, 0, 0)),
        cost_estimate=pl.CostEstimate(
            flops=2 * count * groups * 2 * width * 4 * chans * chans,
            bytes_accessed=2 * (count + 1) * groups * 2 * width * chans + 4 * count * chans * 2 * chans,
            transcendentals=0,
        ),
    )(own, *mates)


def body(records):
    window_count = records.shape[0]
    chans = records.shape[1]
    chan_count = lax.axis_size("chan")
    half_count = chan_count // 2
    time_count = lax.axis_size("tm")
    taper_table = dft_table(records.shape[2], FREQS, FIRST_BIN)
    whitened = whiten(records, taper_table, float(window_count * time_count) ** (-0.25))
    half_freq = FREQS // 2
    lower_half = lax.axis_index("chan") < half_count
    spectra = whitened.reshape(2, half_freq, 2, window_count, chans)

    near = []
    own_h = []
    far_parts = []
    for half in range(2):
        blocks = lax.all_to_all(spectra[half], "tm", split_axis=0, concat_axis=0, tiled=True)
        own_h.append(blocks)
        if half == 0:
            pairs = [(s, s - half_count) for s in range(half_count, chan_count)]
        else:
            pairs = [(s, s + half_count) for s in range(half_count)]
        far_recv = lax.ppermute(blocks, "chan", pairs)
        mates = [blocks] + [shifted(blocks, "chan", -offset) for offset in range(1, half_count)]
        first = pair_stack(blocks, mates[:2] + [far_recv], turn=half == 1)
        far_parts.append(first[2])
        near.append(jnp.concatenate([first[:2]] + [pair_stack(blocks, [mate]) for mate in mates[2:]], axis=0))
    cross_near = jnp.stack(near, axis=0).reshape(1, 2, half_count, chans, 2, chans)

    cross_far = jnp.where(lower_half, far_parts[0], far_parts[1]).reshape(1, chans, 2, chans)
    return (cross_near, cross_far)


def solution(mesh):
    return jax.shard_map(
        body,
        mesh=mesh,
        in_specs=(P("tm", "chan", None),),
        out_specs=(P("tm", None, None, "chan", None, None), P("tm", "chan", None, None)),
        check_vma=False,
    )
```

```python
import functools
import math

import jax
import ml_dtypes
import numpy as np
import jax.numpy as jnp
from jax import lax
from jax.experimental import pallas as pl
from jax.experimental.pallas import tpu as pltpu
from jax.sharding import PartitionSpec as P

FREQS = 64
FIRST_BIN = 32
EPSILON = 1e-06
GROUPS_PER_STEP = 16
WHITEN_ROWS = 1408


def shifted(value, axis, steps):
    count = lax.axis_size(axis)
    pairs = [(source, (source + steps) % count) for source in range(count)]
    return lax.ppermute(value, axis, pairs)


def dft_table(sample_count, frequency_count, first_bin):
    positions = np.arange(sample_count, dtype=np.int64)
    bin_numbers = np.arange(frequency_count, dtype=np.int64) + first_bin
    phase_index = bin_numbers[:, None] * positions[None, :] % sample_count
    phase_angle = 2.0 * math.pi / sample_count * phase_index
    hann_taper = 0.5 - 0.5 * np.cos(2.0 * math.pi / sample_count * positions)
    cosine = hann_taper[None, :] * np.cos(phase_angle)
    sine_part = -hann_taper[None, :] * np.sin(phase_angle)
    table = np.stack([cosine, sine_part], axis=1).reshape(2 * frequency_count, sample_count)
    return jnp.asarray(table.astype(np.float32).astype(ml_dtypes.bfloat16))


def whiten_kernel(scale, table_ref, rows_ref, out_ref):
    spectra = lax.dot_general(
        table_ref[...], rows_ref[...], (((1,), (1,)), ((), ())), preferred_element_type=jnp.float32
    )
    mean_square = jnp.mean(spectra * spectra, axis=0, keepdims=True)
    factor = scale / jnp.sqrt(mean_square + EPSILON)
    out_ref[...] = (spectra * factor).astype(jnp.bfloat16)


def whiten(records, taper_table, overall_scale):
    windows, chans, samples = records.shape
    rows = records.reshape(windows * chans, samples)
    kinds = taper_table.shape[0]
    step = WHITEN_ROWS
    out = pl.pallas_call(
        functools.partial(whiten_kernel, overall_scale),
        out_shape=jax.ShapeDtypeStruct((kinds, windows * chans), jnp.bfloat16),
        grid=(windows * chans // step,),
        in_specs=[
            pl.BlockSpec((kinds, samples), lambda i: (0, 0)),
            pl.BlockSpec((step, samples), lambda i: (i, 0)),
        ],
        out_specs=pl.BlockSpec((kinds, step), lambda i: (0, i)),
        compiler_params=pltpu.CompilerParams(vmem_limit_bytes=48 * 1024 * 1024),
        cost_estimate=pl.CostEstimate(
            flops=2 * kinds * windows * chans * samples,
            bytes_accessed=2 * (windows * chans * samples + kinds * samples + kinds * windows * chans),
            transcendentals=windows * chans,
        ),
    )(taper_table, rows)
    return out.reshape(kinds, windows, chans)


def pair_kernel(group_count, turn, own_ref, *refs):
    mate_refs, out_ref = refs[:-1], refs[-1]
    chans = out_ref.shape[-2]
    contract = (((0,), (0,)), ((), ()))

    @pl.when(pl.program_id(0) == 0)
    def _():
        out_ref[...] = jnp.zeros_like(out_ref)

    for group in range(group_count):
        rows = jnp.concatenate([own_ref[group, 0], own_ref[group, 1]], axis=1)
        for index, mate_ref in enumerate(mate_refs):
            cols = jnp.concatenate([mate_ref[group, 0], mate_ref[group, 1]], axis=1)
            prod = lax.dot_general(rows, cols, contract, preferred_element_type=jnp.float32)
            real = prod[:chans, :chans] + prod[chans:, chans:]
            imag = prod[chans:, :chans] - prod[:chans, chans:]
            both = jnp.concatenate([real, imag], axis=1)
            out_ref[index] += both.astype(jnp.bfloat16).astype(jnp.float32)

    if turn:
        upper = lax.axis_index("chan") >= lax.axis_size("chan") // 2

        @pl.when(jnp.logical_and(upper, pl.program_id(0) == pl.num_programs(0) - 1))
        def _():
            real = out_ref[0, :, :chans]
            imag = out_ref[0, :, chans:]
            out_ref[0] = jnp.concatenate([real.T, -imag.T], axis=1)


def pair_stack(own, mates, turn=False):
    groups, _, width, chans = own.shape
    step = GROUPS_PER_STEP
    spec = pl.BlockSpec((step, 2, width, chans), lambda n: (n, 0, 0, 0))
    count = len(mates)
    return pl.pallas_call(
        functools.partial(pair_kernel, step, turn),
        out_shape=jax.ShapeDtypeStruct((count, chans, 2 * chans), jnp.float32),
        grid=(groups // step,),
        in_specs=[spec] * (count + 1),
        out_specs=pl.BlockSpec((count, chans, 2 * chans), lambda n: (0, 0, 0)),
        cost_estimate=pl.CostEstimate(
            flops=2 * count * groups * 2 * width * 4 * chans * chans,
            bytes_accessed=2 * (count + 1) * groups * 2 * width * chans + 4 * count * chans * 2 * chans,
            transcendentals=0,
        ),
    )(own, *mates)


def body(records):
    window_count = records.shape[0]
    chans = records.shape[1]
    chan_count = lax.axis_size("chan")
    half_count = chan_count // 2
    time_count = lax.axis_size("tm")
    taper_table = dft_table(records.shape[2], FREQS, FIRST_BIN)
    whitened = whiten(records, taper_table, float(window_count * time_count) ** (-0.25))
    half_freq = FREQS // 2
    lower_half = lax.axis_index("chan") < half_count
    spectra = whitened.reshape(2, half_freq, 2, window_count, chans)

    near = []
    own_h = []
    far_recv = []
    for half in range(2):
        blocks = lax.all_to_all(spectra[half], "tm", split_axis=0, concat_axis=0, tiled=True)
        own_h.append(blocks)
        if half == 0:
            pairs = [(s, s - half_count) for s in range(half_count, chan_count)]
        else:
            pairs = [(s, s + half_count) for s in range(half_count)]
        far_recv.append(lax.ppermute(blocks, "chan", pairs))
        mates = [blocks] + [shifted(blocks, "chan", -offset) for offset in range(1, half_count)]
        first = pair_stack(blocks, mates[:2])
        near.append(jnp.concatenate([first] + [pair_stack(blocks, [mate]) for mate in mates[2:]], axis=0))
    cross_near = jnp.stack(near, axis=0).reshape(1, 2, half_count, chans, 2, chans)

    far_own = jnp.where(lower_half, own_h[0], own_h[1])
    far_mate = jnp.where(lower_half, far_recv[0], far_recv[1])
    cross_far = pair_stack(far_own, [far_mate], turn=True).reshape(1, chans, 2, chans)
    return (cross_near, cross_far)


def solution(mesh):
    return jax.shard_map(
        body,
        mesh=mesh,
        in_specs=(P("tm", "chan", None),),
        out_specs=(P("tm", None, None, "chan", None, None), P("tm", "chan", None, None)),
        check_vma=False,
    )
```

```python
import functools
import math

import jax
import ml_dtypes
import numpy as np
import jax.numpy as jnp
from jax import lax
from jax.experimental import pallas as pl
from jax.experimental.pallas import tpu as pltpu
from jax.sharding import PartitionSpec as P

FREQS = 64
FIRST_BIN = 32
EPSILON = 1e-06
GROUPS_PER_STEP = 16
WHITEN_ROWS = 1408


def shifted(value, axis, steps):
    count = lax.axis_size(axis)
    pairs = [(source, (source + steps) % count) for source in range(count)]
    return lax.ppermute(value, axis, pairs)


def dft_table(sample_count, frequency_count, first_bin):
    positions = np.arange(sample_count, dtype=np.int64)
    bin_numbers = np.arange(frequency_count, dtype=np.int64) + first_bin
    phase_index = bin_numbers[:, None] * positions[None, :] % sample_count
    phase_angle = 2.0 * math.pi / sample_count * phase_index
    hann_taper = 0.5 - 0.5 * np.cos(2.0 * math.pi / sample_count * positions)
    cosine = hann_taper[None, :] * np.cos(phase_angle)
    sine_part = -hann_taper[None, :] * np.sin(phase_angle)
    table = np.stack([cosine, sine_part], axis=1).reshape(2 * frequency_count, sample_count)
    return jnp.asarray(table.astype(np.float32).astype(ml_dtypes.bfloat16))


def whiten_kernel(scale, table_ref, rows_ref, out_ref):
    spectra = jnp.dot(rows_ref[...], table_ref[...], preferred_element_type=jnp.float32)
    mean_square = jnp.mean(spectra * spectra, axis=1, keepdims=True)
    factor = scale / jnp.sqrt(mean_square + EPSILON)
    out_ref[...] = (spectra * factor).T.astype(jnp.bfloat16)


def whiten(records, taper_table, overall_scale):
    windows, chans, samples = records.shape
    rows = records.reshape(windows * chans, samples)
    kinds = taper_table.shape[0]
    step = WHITEN_ROWS
    out = pl.pallas_call(
        functools.partial(whiten_kernel, overall_scale),
        out_shape=jax.ShapeDtypeStruct((kinds, windows * chans), jnp.bfloat16),
        grid=(windows * chans // step,),
        in_specs=[
            pl.BlockSpec((samples, kinds), lambda i: (0, 0)),
            pl.BlockSpec((step, samples), lambda i: (i, 0)),
        ],
        out_specs=pl.BlockSpec((kinds, step), lambda i: (0, i)),
        compiler_params=pltpu.CompilerParams(vmem_limit_bytes=48 * 1024 * 1024),
        cost_estimate=pl.CostEstimate(
            flops=2 * kinds * windows * chans * samples,
            bytes_accessed=2 * (windows * chans * samples + kinds * samples + kinds * windows * chans),
            transcendentals=windows * chans,
        ),
    )(taper_table.T, rows)
    return out.reshape(kinds, windows, chans)


def pair_kernel(group_count, turn, own_ref, *refs):
    mate_refs, out_ref = refs[:-1], refs[-1]
    chans = out_ref.shape[-2]
    contract = (((0,), (0,)), ((), ()))

    @pl.when(pl.program_id(0) == 0)
    def _():
        out_ref[...] = jnp.zeros_like(out_ref)

    for group in range(group_count):
        rows = jnp.concatenate([own_ref[group, 0], own_ref[group, 1]], axis=1)
        for index, mate_ref in enumerate(mate_refs):
            cols = jnp.concatenate([mate_ref[group, 0], mate_ref[group, 1]], axis=1)
            prod = lax.dot_general(rows, cols, contract, preferred_element_type=jnp.float32)
            real = prod[:chans, :chans] + prod[chans:, chans:]
            imag = prod[chans:, :chans] - prod[:chans, chans:]
            both = jnp.concatenate([real, imag], axis=1)
            out_ref[index] += both.astype(jnp.bfloat16).astype(jnp.float32)

    if turn:
        upper = lax.axis_index("chan") >= lax.axis_size("chan") // 2

        @pl.when(jnp.logical_and(upper, pl.program_id(0) == pl.num_programs(0) - 1))
        def _():
            real = out_ref[0, :, :chans]
            imag = out_ref[0, :, chans:]
            out_ref[0] = jnp.concatenate([real.T, -imag.T], axis=1)


def pair_stack(own, mates, turn=False):
    groups, _, width, chans = own.shape
    step = GROUPS_PER_STEP
    spec = pl.BlockSpec((step, 2, width, chans), lambda n: (n, 0, 0, 0))
    count = len(mates)
    return pl.pallas_call(
        functools.partial(pair_kernel, step, turn),
        out_shape=jax.ShapeDtypeStruct((count, chans, 2 * chans), jnp.float32),
        grid=(groups // step,),
        in_specs=[spec] * (count + 1),
        out_specs=pl.BlockSpec((count, chans, 2 * chans), lambda n: (0, 0, 0)),
        cost_estimate=pl.CostEstimate(
            flops=2 * count * groups * 2 * width * 4 * chans * chans,
            bytes_accessed=2 * (count + 1) * groups * 2 * width * chans + 4 * count * chans * 2 * chans,
            transcendentals=0,
        ),
    )(own, *mates)


def body(records):
    window_count = records.shape[0]
    chans = records.shape[1]
    chan_count = lax.axis_size("chan")
    half_count = chan_count // 2
    time_count = lax.axis_size("tm")
    taper_table = dft_table(records.shape[2], FREQS, FIRST_BIN)
    whitened = whiten(records, taper_table, float(window_count * time_count) ** (-0.25))
    half_freq = FREQS // 2
    lower_half = lax.axis_index("chan") < half_count
    spectra = whitened.reshape(2, half_freq, 2, window_count, chans)

    near = []
    own_h = []
    far_recv = []
    for half in range(2):
        blocks = lax.all_to_all(spectra[half], "tm", split_axis=0, concat_axis=0, tiled=True)
        own_h.append(blocks)
        if half == 0:
            pairs = [(s, s - half_count) for s in range(half_count, chan_count)]
        else:
            pairs = [(s, s + half_count) for s in range(half_count)]
        far_recv.append(lax.ppermute(blocks, "chan", pairs))
        mates = [blocks] + [shifted(blocks, "chan", -offset) for offset in range(1, half_count)]
        first = pair_stack(blocks, mates[:2])
        near.append(jnp.concatenate([first] + [pair_stack(blocks, [mate]) for mate in mates[2:]], axis=0))
    cross_near = jnp.stack(near, axis=0).reshape(1, 2, half_count, chans, 2, chans)

    far_own = jnp.where(lower_half, own_h[0], own_h[1])
    far_mate = jnp.where(lower_half, far_recv[0], far_recv[1])
    cross_far = pair_stack(far_own, [far_mate], turn=True).reshape(1, chans, 2, chans)
    return (cross_near, cross_far)


def solution(mesh):
    return jax.shard_map(
        body,
        mesh=mesh,
        in_specs=(P("tm", "chan", None),),
        out_specs=(P("tm", None, None, "chan", None, None), P("tm", "chan", None, None)),
        check_vma=False,
    )
```

```python
import functools
import math

import jax
import ml_dtypes
import numpy as np
import jax.numpy as jnp
from jax import lax
from jax.experimental import pallas as pl
from jax.experimental.pallas import tpu as pltpu
from jax.sharding import PartitionSpec as P

FREQS = 64
FIRST_BIN = 32
EPSILON = 1e-06
GROUPS_PER_STEP = 16


def shifted(value, axis, steps):
    count = lax.axis_size(axis)
    pairs = [(source, (source + steps) % count) for source in range(count)]
    return lax.ppermute(value, axis, pairs)


def dft_table(sample_count, frequency_count, first_bin):
    positions = np.arange(sample_count, dtype=np.int64)
    bin_numbers = np.arange(frequency_count, dtype=np.int64) + first_bin
    phase_index = bin_numbers[:, None] * positions[None, :] % sample_count
    phase_angle = 2.0 * math.pi / sample_count * phase_index
    hann_taper = 0.5 - 0.5 * np.cos(2.0 * math.pi / sample_count * positions)
    cosine = hann_taper[None, :] * np.cos(phase_angle)
    sine_part = -hann_taper[None, :] * np.sin(phase_angle)
    table = np.stack([cosine, sine_part], axis=1).reshape(2 * frequency_count, sample_count)
    return jnp.asarray(table.astype(np.float32).astype(ml_dtypes.bfloat16))


def whiten(records, taper_table, overall_scale):
    spectra = jnp.einsum("ks,wcs->kwc", taper_table, records, preferred_element_type=jnp.float32)
    mean_square = jnp.mean(spectra * spectra, axis=0)
    factor = overall_scale / jnp.sqrt(mean_square + EPSILON)
    return (spectra * factor[None]).astype(jnp.bfloat16)


def pair_kernel(group_count, turn, own_ref, *refs):
    if turn:
        mate_refs, final_ref, out_ref = refs[:-2], refs[-2], refs[-1]
    else:
        mate_refs, out_ref = refs[:-1], refs[-1]
    chans = out_ref.shape[-2]
    contract = (((0,), (0,)), ((), ()))

    @pl.when(pl.program_id(0) == 0)
    def _():
        out_ref[...] = jnp.zeros_like(out_ref)

    for group in range(group_count):
        rows = jnp.concatenate([own_ref[group, 0], own_ref[group, 1]], axis=1)
        for index, mate_ref in enumerate(mate_refs):
            cols = jnp.concatenate([mate_ref[group, 0], mate_ref[group, 1]], axis=1)
            prod = lax.dot_general(rows, cols, contract, preferred_element_type=jnp.float32)
            real = prod[:chans, :chans] + prod[chans:, chans:]
            imag = prod[chans:, :chans] - prod[:chans, chans:]
            both = jnp.concatenate([real, imag], axis=1)
            out_ref[index] += both.astype(jnp.bfloat16).astype(jnp.float32)

    if turn:
        upper = lax.axis_index("chan") >= lax.axis_size("chan") // 2
        last = pl.program_id(0) == pl.num_programs(0) - 1

        @pl.when(jnp.logical_and(last, jnp.logical_not(upper)))
        def _():
            final_ref[:, 0, :] = out_ref[0, :, :chans]
            final_ref[:, 1, :] = out_ref[0, :, chans:]

        @pl.when(jnp.logical_and(last, upper))
        def _():
            final_ref[:, 0, :] = out_ref[0, :, :chans].T
            final_ref[:, 1, :] = -out_ref[0, :, chans:].T


def pair_stack(own, mates, turn=False):
    groups, _, width, chans = own.shape
    step = GROUPS_PER_STEP
    spec = pl.BlockSpec((step, 2, width, chans), lambda n: (n, 0, 0, 0))
    count = len(mates)
    total_shape = (count, chans, 2 * chans)
    if turn:
        out_shape = jax.ShapeDtypeStruct((chans, 2, chans), jnp.float32)
        out_spec = pl.BlockSpec((chans, 2, chans), lambda n: (0, 0, 0))
        scratch = [pltpu.VMEM(total_shape, jnp.float32)]
    else:
        out_shape = jax.ShapeDtypeStruct(total_shape, jnp.float32)
        out_spec = pl.BlockSpec(total_shape, lambda n: (0, 0, 0))
        scratch = []
    return pl.pallas_call(
        functools.partial(pair_kernel, step, turn),
        out_shape=out_shape,
        grid=(groups // step,),
        in_specs=[spec] * (count + 1),
        out_specs=out_spec,
        scratch_shapes=scratch,
        cost_estimate=pl.CostEstimate(
            flops=2 * count * groups * 2 * width * 4 * chans * chans,
            bytes_accessed=2 * (count + 1) * groups * 2 * width * chans + 4 * count * chans * 2 * chans,
            transcendentals=0,
        ),
    )(own, *mates)


def body(records):
    window_count = records.shape[0]
    chans = records.shape[1]
    chan_count = lax.axis_size("chan")
    half_count = chan_count // 2
    time_count = lax.axis_size("tm")
    taper_table = dft_table(records.shape[2], FREQS, FIRST_BIN)
    whitened = whiten(records, taper_table, float(window_count * time_count) ** (-0.25))
    half_freq = FREQS // 2
    lower_half = lax.axis_index("chan") < half_count
    spectra = whitened.reshape(2, half_freq, 2, window_count, chans)

    near = []
    own_h = []
    far_recv = []
    for half in range(2):
        blocks = lax.all_to_all(spectra[half], "tm", split_axis=0, concat_axis=0, tiled=True)
        own_h.append(blocks)
        if half == 0:
            pairs = [(s, s - half_count) for s in range(half_count, chan_count)]
        else:
            pairs = [(s, s + half_count) for s in range(half_count)]
        far_recv.append(lax.ppermute(blocks, "chan", pairs))
        mates = [blocks] + [shifted(blocks, "chan", -offset) for offset in range(1, half_count)]
        first = pair_stack(blocks, mates[:2])
        near.append(jnp.concatenate([first] + [pair_stack(blocks, [mate]) for mate in mates[2:]], axis=0))
    cross_near = jnp.stack(near, axis=0).reshape(1, 2, half_count, chans, 2, chans)

    far_own = jnp.where(lower_half, own_h[0], own_h[1])
    far_mate = jnp.where(lower_half, far_recv[0], far_recv[1])
    cross_far = pair_stack(far_own, [far_mate], turn=True).reshape(1, chans, 2, chans)
    return (cross_near, cross_far)


def solution(mesh):
    return jax.shard_map(
        body,
        mesh=mesh,
        in_specs=(P("tm", "chan", None),),
        out_specs=(P("tm", None, None, "chan", None, None), P("tm", "chan", None, None)),
        check_vma=False,
    )
```

```python
import functools
import math

import jax
import ml_dtypes
import numpy as np
import jax.numpy as jnp
from jax import lax
from jax.experimental import pallas as pl
from jax.experimental.pallas import tpu as pltpu
from jax.sharding import PartitionSpec as P

FREQS = 64
FIRST_BIN = 32
EPSILON = 1e-06
GROUPS_PER_STEP = 16


def shifted(value, axis, steps):
    count = lax.axis_size(axis)
    pairs = [(source, (source + steps) % count) for source in range(count)]
    return lax.ppermute(value, axis, pairs)


def dft_table(sample_count, frequency_count, first_bin):
    positions = np.arange(sample_count, dtype=np.int64)
    bin_numbers = np.arange(frequency_count, dtype=np.int64) + first_bin
    phase_index = bin_numbers[:, None] * positions[None, :] % sample_count
    phase_angle = 2.0 * math.pi / sample_count * phase_index
    hann_taper = 0.5 - 0.5 * np.cos(2.0 * math.pi / sample_count * positions)
    cosine = hann_taper[None, :] * np.cos(phase_angle)
    sine_part = -hann_taper[None, :] * np.sin(phase_angle)
    table = np.stack([cosine, sine_part], axis=1).reshape(2 * frequency_count, sample_count)
    return jnp.asarray(table.astype(np.float32).astype(ml_dtypes.bfloat16))


def whiten(records, taper_table, overall_scale):
    spectra = jnp.einsum("ks,wcs->kwc", taper_table, records, preferred_element_type=jnp.float32)
    mean_square = jnp.mean(spectra * spectra, axis=0)
    factor = overall_scale / jnp.sqrt(mean_square + EPSILON)
    return (spectra * factor[None]).astype(jnp.bfloat16)


def pair_kernel(group_count, turn, own_ref, *refs):
    if turn:
        mate_refs, final_ref, out_ref = refs[:-2], refs[-2], refs[-1]
    else:
        mate_refs, out_ref = refs[:-1], refs[-1]
    chans = out_ref.shape[-2]
    contract = (((0,), (0,)), ((), ()))

    @pl.when(pl.program_id(0) == 0)
    def _():
        out_ref[...] = jnp.zeros_like(out_ref)

    for group in range(group_count):
        rows = jnp.concatenate([own_ref[group, 0], own_ref[group, 1]], axis=1)
        for index, mate_ref in enumerate(mate_refs):
            if turn:
                cols = jnp.concatenate([mate_ref[0, :, group, :], mate_ref[1, :, group, :]], axis=1)
            else:
                cols = jnp.concatenate([mate_ref[group, 0], mate_ref[group, 1]], axis=1)
            prod = lax.dot_general(rows, cols, contract, preferred_element_type=jnp.float32)
            real = prod[:chans, :chans] + prod[chans:, chans:]
            imag = prod[chans:, :chans] - prod[:chans, chans:]
            both = jnp.concatenate([real, imag], axis=1)
            out_ref[index] += both.astype(jnp.bfloat16).astype(jnp.float32)

    if turn:
        upper = lax.axis_index("chan") >= lax.axis_size("chan") // 2
        last = pl.program_id(0) == pl.num_programs(0) - 1

        @pl.when(jnp.logical_and(last, jnp.logical_not(upper)))
        def _():
            final_ref[:, 0, :] = out_ref[0, :, :chans]
            final_ref[:, 1, :] = out_ref[0, :, chans:]

        @pl.when(jnp.logical_and(last, upper))
        def _():
            final_ref[:, 0, :] = out_ref[0, :, :chans].T
            final_ref[:, 1, :] = -out_ref[0, :, chans:].T


def pair_stack(own, mates, turn=False):
    groups, _, width, chans = own.shape
    step = GROUPS_PER_STEP
    spec = pl.BlockSpec((step, 2, width, chans), lambda n: (n, 0, 0, 0))
    count = len(mates)
    total_shape = (count, chans, 2 * chans)
    mate_spec = spec
    if turn:
        mates = [mate.transpose(1, 2, 0, 3) for mate in mates]
        mate_spec = pl.BlockSpec((2, width, step, chans), lambda n: (0, 0, n, 0))
        out_shape = jax.ShapeDtypeStruct((chans, 2, chans), jnp.float32)
        out_spec = pl.BlockSpec((chans, 2, chans), lambda n: (0, 0, 0))
        scratch = [pltpu.VMEM(total_shape, jnp.float32)]
    else:
        out_shape = jax.ShapeDtypeStruct(total_shape, jnp.float32)
        out_spec = pl.BlockSpec(total_shape, lambda n: (0, 0, 0))
        scratch = []
    return pl.pallas_call(
        functools.partial(pair_kernel, step, turn),
        out_shape=out_shape,
        grid=(groups // step,),
        in_specs=[spec] + [mate_spec] * count,
        out_specs=out_spec,
        scratch_shapes=scratch,
        cost_estimate=pl.CostEstimate(
            flops=2 * count * groups * 2 * width * 4 * chans * chans,
            bytes_accessed=2 * (count + 1) * groups * 2 * width * chans + 4 * count * chans * 2 * chans,
            transcendentals=0,
        ),
    )(own, *mates)


def body(records):
    window_count = records.shape[0]
    chans = records.shape[1]
    chan_count = lax.axis_size("chan")
    half_count = chan_count // 2
    time_count = lax.axis_size("tm")
    taper_table = dft_table(records.shape[2], FREQS, FIRST_BIN)
    whitened = whiten(records, taper_table, float(window_count * time_count) ** (-0.25))
    half_freq = FREQS // 2
    lower_half = lax.axis_index("chan") < half_count
    spectra = whitened.reshape(2, half_freq, 2, window_count, chans)

    near = []
    own_h = []
    far_recv = []
    for half in range(2):
        blocks = lax.all_to_all(spectra[half], "tm", split_axis=0, concat_axis=0, tiled=True)
        own_h.append(blocks)
        if half == 0:
            pairs = [(s, s - half_count) for s in range(half_count, chan_count)]
        else:
            pairs = [(s, s + half_count) for s in range(half_count)]
        far_recv.append(lax.ppermute(blocks, "chan", pairs))
        mates = [blocks] + [shifted(blocks, "chan", -offset) for offset in range(1, half_count)]
        first = pair_stack(blocks, mates[:2])
        near.append(jnp.concatenate([first] + [pair_stack(blocks, [mate]) for mate in mates[2:]], axis=0))
    cross_near = jnp.stack(near, axis=0).reshape(1, 2, half_count, chans, 2, chans)

    far_own = jnp.where(lower_half, own_h[0], own_h[1])
    far_mate = jnp.where(lower_half, far_recv[0], far_recv[1])
    cross_far = pair_stack(far_own, [far_mate], turn=True).reshape(1, chans, 2, chans)
    return (cross_near, cross_far)


def solution(mesh):
    return jax.shard_map(
        body,
        mesh=mesh,
        in_specs=(P("tm", "chan", None),),
        out_specs=(P("tm", None, None, "chan", None, None), P("tm", "chan", None, None)),
        check_vma=False,
    )
```

```python
import functools
import math

import jax
import ml_dtypes
import numpy as np
import jax.numpy as jnp
from jax import lax
from jax.experimental import pallas as pl
from jax.experimental.pallas import tpu as pltpu
from jax.sharding import PartitionSpec as P

FREQS = 64
FIRST_BIN = 32
EPSILON = 1e-06
GROUPS_PER_STEP = 16


def shifted(value, axis, steps):
    count = lax.axis_size(axis)
    pairs = [(source, (source + steps) % count) for source in range(count)]
    return lax.ppermute(value, axis, pairs)


def dft_table(sample_count, frequency_count, first_bin):
    positions = np.arange(sample_count, dtype=np.int64)
    bin_numbers = np.arange(frequency_count, dtype=np.int64) + first_bin
    phase_index = bin_numbers[:, None] * positions[None, :] % sample_count
    phase_angle = 2.0 * math.pi / sample_count * phase_index
    hann_taper = 0.5 - 0.5 * np.cos(2.0 * math.pi / sample_count * positions)
    cosine = hann_taper[None, :] * np.cos(phase_angle)
    sine_part = -hann_taper[None, :] * np.sin(phase_angle)
    table = np.stack([cosine, sine_part], axis=1).reshape(2 * frequency_count, sample_count)
    return jnp.asarray(table.astype(np.float32).astype(ml_dtypes.bfloat16))


def whiten(records, taper_table, overall_scale):
    spectra = jnp.einsum("ks,wcs->kwc", taper_table, records, preferred_element_type=jnp.float32)
    mean_square = jnp.mean(spectra * spectra, axis=0)
    factor = overall_scale / jnp.sqrt(mean_square + EPSILON)
    return (spectra * factor[None]).astype(jnp.bfloat16)


def pair_kernel(group_count, turn, own_ref, *refs):
    if turn:
        mate_refs, final_ref, out_ref = refs[:-2], refs[-2], refs[-1]
    else:
        mate_refs, out_ref = refs[:-1], refs[-1]
    chans = out_ref.shape[-2]
    contract = (((0,), (0,)), ((), ()))

    @pl.when(pl.program_id(0) == 0)
    def _():
        out_ref[...] = jnp.zeros_like(out_ref)

    for group in range(group_count):
        rows = jnp.concatenate([own_ref[group, 0], own_ref[group, 1]], axis=1)
        if turn:
            lower = lax.axis_index("chan") < lax.axis_size("chan") // 2
            pairs = [[jnp.concatenate([ref[0, :, group, :], ref[1, :, group, :]], axis=1) for ref in mate_refs]]
            pairs = [jnp.where(lower, pairs[0][0], pairs[0][1])]
        else:
            pairs = [jnp.concatenate([ref[group, 0], ref[group, 1]], axis=1) for ref in mate_refs]
        for index, cols in enumerate(pairs):
            prod = lax.dot_general(rows, cols, contract, preferred_element_type=jnp.float32)
            real = prod[:chans, :chans] + prod[chans:, chans:]
            imag = prod[chans:, :chans] - prod[:chans, chans:]
            both = jnp.concatenate([real, imag], axis=1)
            out_ref[index] += both.astype(jnp.bfloat16).astype(jnp.float32)

    if turn:
        upper = lax.axis_index("chan") >= lax.axis_size("chan") // 2
        last = pl.program_id(0) == pl.num_programs(0) - 1

        @pl.when(jnp.logical_and(last, jnp.logical_not(upper)))
        def _():
            final_ref[:, 0, :] = out_ref[0, :, :chans]
            final_ref[:, 1, :] = out_ref[0, :, chans:]

        @pl.when(jnp.logical_and(last, upper))
        def _():
            final_ref[:, 0, :] = out_ref[0, :, :chans].T
            final_ref[:, 1, :] = -out_ref[0, :, chans:].T


def pair_stack(own, mates, turn=False):
    groups, _, width, chans = own.shape
    step = GROUPS_PER_STEP
    spec = pl.BlockSpec((step, 2, width, chans), lambda n: (n, 0, 0, 0))
    count = len(mates)
    total_shape = (count, chans, 2 * chans)
    mate_spec = spec
    if turn:
        count = 1
        total_shape = (count, chans, 2 * chans)
        mates = [mate.transpose(1, 2, 0, 3) for mate in mates]
        mate_spec = pl.BlockSpec((2, width, step, chans), lambda n: (0, 0, n, 0))
        out_shape = jax.ShapeDtypeStruct((chans, 2, chans), jnp.float32)
        out_spec = pl.BlockSpec((chans, 2, chans), lambda n: (0, 0, 0))
        scratch = [pltpu.VMEM(total_shape, jnp.float32)]
    else:
        out_shape = jax.ShapeDtypeStruct(total_shape, jnp.float32)
        out_spec = pl.BlockSpec(total_shape, lambda n: (0, 0, 0))
        scratch = []
    return pl.pallas_call(
        functools.partial(pair_kernel, step, turn),
        out_shape=out_shape,
        grid=(groups // step,),
        in_specs=[spec] + [mate_spec] * len(mates),
        out_specs=out_spec,
        scratch_shapes=scratch,
        cost_estimate=pl.CostEstimate(
            flops=2 * count * groups * 2 * width * 4 * chans * chans,
            bytes_accessed=2 * (count + 1) * groups * 2 * width * chans + 4 * count * chans * 2 * chans,
            transcendentals=0,
        ),
    )(own, *mates)


def body(records):
    window_count = records.shape[0]
    chans = records.shape[1]
    chan_count = lax.axis_size("chan")
    half_count = chan_count // 2
    time_count = lax.axis_size("tm")
    taper_table = dft_table(records.shape[2], FREQS, FIRST_BIN)
    whitened = whiten(records, taper_table, float(window_count * time_count) ** (-0.25))
    half_freq = FREQS // 2
    lower_half = lax.axis_index("chan") < half_count
    spectra = whitened.reshape(2, half_freq, 2, window_count, chans)

    near = []
    own_h = []
    far_recv = []
    for half in range(2):
        blocks = lax.all_to_all(spectra[half], "tm", split_axis=0, concat_axis=0, tiled=True)
        own_h.append(blocks)
        if half == 0:
            pairs = [(s, s - half_count) for s in range(half_count, chan_count)]
        else:
            pairs = [(s, s + half_count) for s in range(half_count)]
        far_recv.append(lax.ppermute(blocks, "chan", pairs))
        mates = [blocks] + [shifted(blocks, "chan", -offset) for offset in range(1, half_count)]
        first = pair_stack(blocks, mates[:2])
        near.append(jnp.concatenate([first] + [pair_stack(blocks, [mate]) for mate in mates[2:]], axis=0))
    cross_near = jnp.stack(near, axis=0).reshape(1, 2, half_count, chans, 2, chans)

    far_own = jnp.where(lower_half, own_h[0], own_h[1])
    cross_far = pair_stack(far_own, far_recv, turn=True).reshape(1, chans, 2, chans)
    return (cross_near, cross_far)


def solution(mesh):
    return jax.shard_map(
        body,
        mesh=mesh,
        in_specs=(P("tm", "chan", None),),
        out_specs=(P("tm", None, None, "chan", None, None), P("tm", "chan", None, None)),
        check_vma=False,
    )
```
